32 devices in a mesh: groups: 2 (over x), along: 8 (over z, y), across: 2 (over core).
Axes of the slice: x: 2, y: 2, z: 4, core: 2. Of those that a mesh axis runs over, the one named last changes fastest.
Arguments:
- toa_bands: bfloat16 [1024, 4, 2048], P(('groups', 'along'), None, 'across'), parts along dimension 0, may hold values from 0.019897461 to 0.59765625
- dark_mask: int32 [1024, 2048], P(('groups', 'along'), 'across'), parts along dimension 0, may hold values 0 or 1
- vapour: float32 [1024, 2048], P(('groups', 'along'), 'across'), parts along dimension 0, may hold values from 0 to 7
- elev_class: int32 [1024, 2048], P(('groups', 'along'), 'across'), parts along dimension 0, may hold values from 0 to 6
- elev_frac: float32 [1024, 2048], P(('groups', 'along'), 'across'), parts along dimension 0, may hold values from 0 to 1
- kernel: float32 [61], replicated, may hold values from 0.1 to 1
- lut_gain: bfloat16 [4, 8, 16, 8], replicated, may hold values from 1 to 2
- lut_path: bfloat16 [4, 8, 16, 8], replicated, may hold values from 0 to 0.29882812
- lut_albedo: bfloat16 [4, 8, 16, 8], replicated, may hold values from 0.049804688 to 0.25
- routes: int32 [64, 2], P(('groups', 'along')), parts along dimension 0, may hold values from 0 to 7, as said below
- starts: int32 [64, 2], P(('groups', 'along')), parts along dimension 0, may hold values from 0 to 48
Outputs:
- tile_out: bfloat16 [16, 64, 4, 2048], P(('groups', 'along'), None, None, 'across'), parts along dimension 0
The draws below stay inside these ranges and needn't reach their ends.
There are 2 independent parts, one for each index of `groups`. The reference program is written for one: setup_inputs(seed, part) draws one part's arguments, and reference() takes and returns one part's arrays. A program takes and returns all parts, laid end to end along the dimension named above; an argument that names none is the same for every part. Nothing has to cross between parts.
Inputs may be any that keep to these rules, and one draw needn't show every extreme that they name: `dark_mask`: 1 marks a dark pixel. `elev_class`: the class and the next one are both classes of the table. `routes`: the first block of segment s is s // 4, the block of the segment's own rows; the second lies 1 to 2 blocks before or after it; among the 4 segments of one device at most 2 have their second block at any one signed distance, and in every draw some device has exactly 2 at some distance.
All inputs are finite; a program needn't handle non-finite values. No bound on the sum of `dark_mask` on one device may be relied on, other than what follows from the above.
Results may differ from the reference program's by a relative error of at most 0.0043.
Values may be sent and summed in bfloat16 or wider, within the bound.
A program may use at most 64 MiB of HBM per device.

```python
import math
import jax
import jax.numpy as jnp
from jax import lax

BANDS = 4
NA = 16
NW = 8
NE = 8
HALO = 30
SEG = 16
REACH = 2
ROW_DEV = 64
NR = 512
NC = 2048
SEG_DEV = 4
CAP = 2
NSEGS = 32
TILES = 8
TILE_ROWS = 64


def draw_routes(key, part):
    key_full = jax.random.fold_in(key, 101)
    key_slots = jax.random.fold_in(key, 202)
    key_order = jax.random.fold_in(key, 303)
    side_count = 2 * REACH
    side_ids = jnp.arange(side_count, dtype=jnp.int32)
    side_value = jnp.where(side_ids < REACH, side_ids - REACH, side_ids - REACH + 1)
    devices = jnp.arange(TILES, dtype=jnp.int32)
    dest = devices[:, None] + side_value[None, :]
    valid = (dest >= 0) & (dest < TILES)
    full_score = jax.random.randint(key_full, (TILES, side_count), 0, 1 << 16) * side_count + side_ids[None, :]
    full_side = jnp.argmax(jnp.where(valid, full_score, -1), axis=1).astype(jnp.int32)
    slot_ids = jnp.arange(side_count * CAP, dtype=jnp.int32)
    slot_side = slot_ids // CAP
    slot_score = jax.random.randint(key_slots, (TILES, side_count * CAP), 0, 1 << 16) * (side_count * CAP) + slot_ids[None, :]
    slot_valid = valid[:, slot_side]
    order_key = slot_score + (1 << 23) * (slot_side[None, :] != full_side[:, None]).astype(jnp.int32) + (1 << 25) * (1 - slot_valid.astype(jnp.int32))
    order = jnp.argsort(order_key, axis=1)[:, :SEG_DEV]
    chosen_side = slot_side[order]
    mix_score = jax.random.randint(key_order, (TILES, SEG_DEV), 0, 1 << 16) * SEG_DEV + jnp.arange(SEG_DEV, dtype=jnp.int32)[None, :]
    mix = jnp.argsort(mix_score, axis=1)
    chosen_side = jnp.take_along_axis(chosen_side, mix, axis=1)
    second = devices[:, None] + side_value[chosen_side]
    first = jnp.broadcast_to(devices[:, None], (TILES, SEG_DEV))
    return jnp.stack([first, second], axis=-1).reshape(NSEGS, 2).astype(jnp.int32)


def set_ends(entries, own_key, smallest, largest):
    shape = entries.shape
    index_at = [jax.random.randint(jax.random.fold_in(own_key, axis), (), 0, shape[axis]) for axis in range(len(shape))]
    entries = entries.at[tuple(index_at)].set(smallest)
    longest = shape.index(max(shape))
    index_at[longest] = (index_at[longest] + 1) % shape[longest]
    return entries.at[tuple(index_at)].set(largest)


def block_scale(rng, extent, split, least, top_value):
    gain = 1.0
    for position, parts in split:
        draws = jax.random.uniform(jax.random.fold_in(jax.random.fold_in(rng, 6), position), (parts,), jnp.float32, least / len(split), top_value / len(split))
        gain = gain * jnp.repeat(jnp.exp(draws), extent[position] // parts).reshape((-1,) + (1,) * (len(extent) - 1 - position))
    return gain


def setup_inputs(seed: int = 0, part: int = 0) -> dict:
    keys = jax.random.split(jax.random.key(seed), 12)
    part_splits = jax.random.split(jax.random.fold_in(keys[11], part), 12)
    return {
        "toa_bands": jnp.clip(0.019897461 + 0.5777588 * jax.random.uniform(part_splits[0], (NR, BANDS, NC), jnp.float32) ** block_scale(part_splits[0], (NR, BANDS, NC), ((0, 8), (2, 2)), -0.2, 0.2), 0.019897461, 0.59765625).astype(jnp.bfloat16),
        "dark_mask": set_ends((jax.random.randint(part_splits[1], (NR, NC), 0, 1024) < 1).astype(jnp.int32), jax.random.fold_in(part_splits[1], 1), 0, 1),
        "vapour": jnp.clip(7.0 * jax.random.uniform(part_splits[2], (NR, NC), jnp.float32) ** block_scale(part_splits[2], (NR, NC), ((0, 8), (1, 2)), -0.2, 0.2), 0.0, 7.0),
        "elev_class": set_ends(jax.random.randint(part_splits[3], (NR, NC), 0, NE - 1), jax.random.fold_in(part_splits[3], 1), 0, (NE - 1) - 1).astype(jnp.int32),
        "elev_frac": jnp.clip(1.0 * jax.random.uniform(part_splits[4], (NR, NC), jnp.float32) ** block_scale(part_splits[4], (NR, NC), ((0, 8), (1, 2)), -0.2, 0.2), 0.0, 1.0),
        "kernel": jnp.clip(jnp.exp(jax.random.uniform(keys[5], (2 * HALO + 1,), jnp.float32, math.log(0.1), math.log(1.0))), 0.1, 1.0),
        "lut_gain": jnp.clip(jax.random.uniform(keys[6], (BANDS, NE, NA, NW), jnp.float32, 1.0, 2.0), 1.0, 2.0).astype(jnp.bfloat16),
        "lut_path": jnp.clip(jax.random.uniform(keys[7], (BANDS, NE, NA, NW), jnp.float32, 0.0, 0.29882812), 0.0, 0.29882812).astype(jnp.bfloat16),
        "lut_albedo": jnp.clip(jax.random.uniform(keys[8], (BANDS, NE, NA, NW), jnp.float32, 0.049804688, 0.25), 0.049804688, 0.25).astype(jnp.bfloat16),
        "routes": draw_routes(jax.random.fold_in(jax.random.fold_in(keys[11], part), 71), part),
        "starts": set_ends(jax.random.randint(part_splits[10], (NSEGS, 2), 0, TILE_ROWS - SEG + 1), jax.random.fold_in(part_splits[10], 1), 0, TILE_ROWS - SEG).astype(jnp.int32),
    }


def smooth_axis(fields, kernel, axis):
    size = fields.shape[axis]
    tap_count = kernel.shape[0]
    half_width = tap_count // 2
    padding = [(0, 0), (0, 0), (0, 0)]
    padding[axis] = (half_width, half_width)
    padded = jnp.pad(fields, padding)
    total = jnp.zeros_like(fields)
    for tap in range(tap_count):
        total = total + kernel[tap] * lax.slice_in_dim(padded, tap, tap + size, axis=axis)
    return total


def correct_block(inputs, lut_table):
    toa_block, aero_pos, vapour_block, class_block, frac_block = inputs
    a_low = jnp.clip(jnp.floor(aero_pos).astype(jnp.int32), 0, NA - 2)
    a_frac = aero_pos - a_low.astype(aero_pos.dtype)
    w_low = jnp.clip(jnp.floor(vapour_block).astype(jnp.int32), 0, NW - 2)
    w_frac = vapour_block - w_low.astype(vapour_block.dtype)
    coefficient = jnp.zeros((lut_table.shape[0],) + aero_pos.shape, dtype=jnp.float32)
    for e_step in range(2):
        elev_weight = frac_block if e_step == 1 else 1.0 - frac_block
        for a_step in range(2):
            a_weight = a_frac if a_step == 1 else 1.0 - a_frac
            for w_step in range(2):
                w_weight = w_frac if w_step == 1 else 1.0 - w_frac
                joint_weight = (a_weight * w_weight).astype(jnp.bfloat16)
                joint_weight = lax.optimization_barrier(joint_weight).astype(jnp.float32)
                flat_index = ((class_block + e_step) * NA + a_low + a_step) * NW + w_low + w_step
                values = jnp.take(lut_table, flat_index.reshape(-1).astype(jnp.int32), axis=1)
                values = values.reshape((lut_table.shape[0],) + aero_pos.shape)
                coefficient = coefficient + (elev_weight * joint_weight)[None] * values
    coefficient = coefficient.reshape((BANDS, 3) + aero_pos.shape)
    radiance = jnp.transpose(toa_block.astype(jnp.float32), (1, 0, 2))
    scaled = coefficient[:, 0] * radiance - coefficient[:, 1]
    surface = scaled / (1.0 + coefficient[:, 2] * scaled)
    return jnp.transpose(surface, (1, 0, 2)).astype(jnp.bfloat16)


def reference(toa_bands, dark_mask, vapour, elev_class, elev_frac, kernel, lut_gain, lut_path, lut_albedo, routes, starts):
    darkness = dark_mask.astype(jnp.float32)
    blue_band = toa_bands[:, 0, :].astype(jnp.float32)
    red_band = toa_bands[:, 2, :].astype(jnp.float32)
    fields = jnp.stack([darkness * 8.0 * (blue_band - 0.5 * red_band), darkness])
    smoothed = smooth_axis(smooth_axis(fields, kernel, 1), kernel, 2)
    aerosol = smoothed[0] / jnp.maximum(smoothed[1], 1.0)
    aero_pos = (NA - 1) * jax.nn.sigmoid(aerosol)
    lut_table = jnp.stack([lut_gain, lut_path, lut_albedo], axis=1).astype(jnp.float32).reshape(BANDS * 3, NE * NA * NW)
    block_count = NR // ROW_DEV
    inputs = (toa_bands.reshape(block_count, ROW_DEV, BANDS, NC),
              aero_pos.reshape(block_count, ROW_DEV, NC),
              vapour.reshape(block_count, ROW_DEV, NC),
              elev_class.reshape(block_count, ROW_DEV, NC),
              elev_frac.reshape(block_count, ROW_DEV, NC))
    corrected = lax.map(lambda item: correct_block(item, lut_table), inputs).reshape(NR, BANDS, NC)
    segment_rows = corrected.reshape(NSEGS * SEG, BANDS * NC).astype(jnp.float32)
    summed = jnp.zeros((TILES * TILE_ROWS, BANDS * NC), dtype=jnp.float32)
    counts = jnp.zeros((TILES * TILE_ROWS,), dtype=jnp.float32)
    for route_slot in range(2):
        target = routes[:, route_slot][:, None] * TILE_ROWS + starts[:, route_slot][:, None] + jnp.arange(SEG, dtype=jnp.int32)[None, :]
        target = target.reshape(-1).astype(jnp.int32)
        summed = summed.at[target].add(segment_rows)
        counts = counts.at[target].add(jnp.ones((NSEGS * SEG,), dtype=jnp.float32))
    tile_out = (summed / jnp.maximum(counts, 1.0)[:, None]).astype(jnp.bfloat16)
    return tile_out.reshape(TILES, TILE_ROWS, BANDS, NC)
```

```python
import functools
import math

import jax
import jax.numpy as jnp
from jax import lax
from jax.experimental import pallas as pl
from jax.experimental.pallas import tpu as pltpu
from jax.sharding import PartitionSpec as P

SEG = 16
REACH = 2
CAP = 2
LANES = 128
WIDTH = 128
MESH_ID = pl.DeviceIdType.MESH
SIDES = [side - REACH for side in range(REACH)] + [side + 1 for side in range(REACH)]
LAG = 8
f32 = jnp.float32
bf16 = jnp.bfloat16


def split(value):
    high = value.astype(bf16)
    return high, (value - high.astype(f32)).astype(bf16)


def toeplitz(taps, row_count, width, first):
    line = jnp.broadcast_to(taps, (8, taps.shape[1]))
    if width > taps.shape[1]:
        line = jnp.concatenate([line, jnp.zeros((8, width - taps.shape[1]), f32)], axis=1)
    stair = pltpu.roll(line, 0, 1, stride=1, stride_axis=0)
    return jnp.concatenate(
        [pltpu.roll(stair, first + 8 * group, 1) for group in range(row_count // 8)], axis=0
    )


def dot_nt(left, right):
    return lax.dot_general(left, right, (((1,), (1,)), ((), ())), preferred_element_type=f32)


def exists(position, count):
    return (position >= 0) & (position < count)


def main_kernel(
    n_along,
    n_across,
    bands,
    levels,
    routes_hbm,
    starts_hbm,
    toa_hbm,
    mask_hbm,
    taps_hbm,
    gain_hbm,
    path_hbm,
    albedo_hbm,
    vapour_hbm,
    class_hbm,
    frac_hbm,
    out_ref,
    routes_ref,
    starts_ref,
    raw_ref,
    mask_ref,
    taps_ref,
    gain_ref,
    path_ref,
    albedo_ref,
    vapour_ref,
    class_ref,
    frac_ref,
    toa_ref,
    tags_ref,
    taps_pad,
    padded,
    tall,
    pos_ref,
    weights,
    heights,
    corrected,
    slots,
    got_rows,
    got_tags,
    place,
    scale,
    load_sem,
    halo_send,
    halo_recv,
    side_send,
    side_recv,
    tag_send,
    tag_recv,
    slot_send,
    slot_recv,
):
    along, across = lax.axis_index("along"), lax.axis_index("across")
    levels_e, levels_a, levels_w = levels
    rows, _, cols = toa_hbm.shape
    halo = (padded.shape[0] - rows) // 2
    half = taps_hbm.shape[1] // 2
    width = slots.shape[2]
    chunks = cols // width
    seg_rows = SEG * bands
    seg_dev = rows // SEG
    own_rows = rows * bands
    pair = 2 * width
    mirror = across % 2
    inner = across + 1 - 2 * mirror
    outer = across - 1 + 2 * mirror
    pieces = halo_send.shape[1]
    per_piece = chunks // pieces

    def lanes_of(chunk):
        at = jnp.where(mirror == 0, chunk, chunks - 1 - chunk) * width
        return pl.ds(pl.multiple_of(at, width), width)

    loads = [
        pltpu.make_async_copy(source, target, load_sem.at[number])
        for number, (source, target) in enumerate(
            (
                (routes_hbm, routes_ref),
                (starts_hbm, starts_ref),
                (toa_hbm, raw_ref),
                (mask_hbm, mask_ref),
                (taps_hbm, taps_ref),
                (gain_hbm, gain_ref),
                (path_hbm, path_ref),
                (albedo_hbm, albedo_ref),
                (vapour_hbm, vapour_ref),
                (class_hbm, class_ref),
                (frac_hbm, frac_ref),
            )
        )
    ]
    for load in loads[:4]:
        load.start()
    barrier = pltpu.get_barrier_semaphore()
    peers = [
        (exists(along + da, n_along), {"along": along + da})
        for da in sorted({-1, 1, *SIDES}, key=abs)
    ]
    peers += [
        (exists(inner, n_across), {"across": inner}),
        (exists(outer, n_across), {"across": outer}),
    ]
    for present, peer in peers:

        @pl.when(present)
        def _():
            pl.semaphore_signal(barrier, inc=1, device_id=peer, device_id_type=MESH_ID)

    row = lax.broadcasted_iota(jnp.int32, (rows, rows * bands), 0) * bands
    col = lax.broadcasted_iota(jnp.int32, (rows, rows * bands), 1)
    pick = jnp.where(col == row, 8.0, 0.0) + jnp.where(col == row + 2, -4.0, 0.0)
    for load in loads[:4]:
        load.wait()
    for load in loads[4:]:
        load.start()
    flat = raw_ref[...].astype(f32).reshape(rows * bands, cols).astype(bf16)
    toa_ref[...] = flat
    value = jnp.dot(pick.astype(bf16), flat, preferred_element_type=f32)
    darkness = mask_ref[...].astype(f32)
    weighted = (darkness * value).astype(bf16)
    darkness = darkness.astype(bf16)
    for tile in range(chunks):
        own = slice(tile * width, (tile + 1) * width)
        at = pl.multiple_of((jnp.where(mirror == 0, tile, chunks - 1 - tile) + 1) * pair, pair)
        padded[halo : halo + rows, pl.ds(at, width)] = weighted[:, own]
        padded[halo : halo + rows, pl.ds(at + width, width)] = darkness[:, own]

    lane = lax.broadcasted_iota(jnp.int32, (8, CAP * seg_rows), 1)
    for number, side in enumerate(SIDES):
        target = jnp.full((8, CAP * seg_rows), -1, jnp.int32)
        rank = jnp.int32(0)
        for s in range(seg_dev):
            hit = routes_ref[1, s] - along == side
            spot = jnp.where(hit, rank, -1)
            inside = (lane >= spot * seg_rows) & (lane < (spot + 1) * seg_rows) & (spot >= 0)
            target = jnp.where(inside, starts_ref[1, s] * bands + lane - spot * seg_rows, target)
            rank = rank + jnp.where(hit, 1, 0)
        tags_ref[number] = target.astype(f32)

    spans = {
        -1: (slice(halo, 2 * halo), slice(halo + rows, 2 * halo + rows)),
        1: (slice(rows, halo + rows), slice(0, halo)),
    }

    def halo_copy(index, piece):
        da = (-1, 1)[index]
        begin = (1 + piece * per_piece) * pair
        at = slice(begin, begin + per_piece * pair)
        return pltpu.make_async_remote_copy(
            src_ref=padded.at[spans[da][0], at],
            dst_ref=padded.at[spans[da][1], at],
            send_sem=halo_send.at[index, piece],
            recv_sem=halo_recv.at[index, piece],
            device_id={"along": along + da},
            device_id_type=MESH_ID,
        )

    def side_copy(index):
        source, target = ((chunks, chunks + 1), (1, 0))[index]
        return pltpu.make_async_remote_copy(
            src_ref=padded.at[:, source * pair : (source + 1) * pair],
            dst_ref=padded.at[:, target * pair : (target + 1) * pair],
            send_sem=side_send.at[index],
            recv_sem=side_recv.at[index],
            device_id={"across": (inner, outer)[index]},
            device_id_type=MESH_ID,
        )

    def tag_copy(number):
        return pltpu.make_async_remote_copy(
            src_ref=tags_ref.at[number],
            dst_ref=got_tags.at[number],
            send_sem=tag_send.at[number],
            recv_sem=tag_recv.at[number],
            device_id={"along": along + SIDES[number]},
            device_id_type=MESH_ID,
        )

    def slot_copy(chunk, number):
        count = CAP * seg_rows
        return pltpu.make_async_remote_copy(
            src_ref=slots.at[chunk, number * count : (number + 1) * count],
            dst_ref=got_rows.at[chunk, number * count : (number + 1) * count],
            send_sem=slot_send.at[chunk, number],
            recv_sem=slot_recv.at[chunk, number],
            device_id={"along": along + SIDES[number]},
            device_id_type=MESH_ID,
        )

    def start_halo(piece):
        for index, da in enumerate((-1, 1)):

            @pl.when(exists(along + da, n_along))
            def _():
                halo_copy(index, piece).start()

    pl.semaphore_wait(barrier, sum(present.astype(jnp.int32) for present, _ in peers))
    start_halo(0)
    order = sorted(range(len(SIDES)), key=lambda number: abs(SIDES[number]))
    for number in order:

        @pl.when(exists(along + SIDES[number], n_along))
        def _():
            tag_copy(number).start()

        @pl.when(jnp.logical_not(exists(along - SIDES[number], n_along)))
        def _():
            begin = number * CAP * seg_rows
            got_rows[:, begin : begin + CAP * seg_rows, :] = jnp.zeros(
                (chunks, CAP * seg_rows, width), bf16
            )
            got_tags[number] = jnp.full(got_tags.shape[1:], -1.0, f32)

    for da in (-1, 1):

        @pl.when(jnp.logical_not(exists(along - da, n_along)))
        def _():
            padded[spans[da][1], pair : (chunks + 1) * pair] = jnp.zeros(
                (halo, chunks * pair), bf16
            )

    for index, (peer, target) in enumerate(((inner, chunks + 1), (outer, 0))):

        @pl.when(jnp.logical_not(exists(peer, n_across)))
        def _():
            padded[:, target * pair : (target + 1) * pair] = jnp.zeros(
                (padded.shape[0], pair), bf16
            )

    for load in loads[4:8]:
        load.wait()
    taps_pad[...] = jnp.zeros(taps_pad.shape, f32)
    taps_pad[0:1, 0 : taps_ref.shape[1]] = taps_ref[...]
    taps = taps_pad[0:1, :]
    down = jnp.concatenate(split(toeplitz(taps, rows, 2 * halo + rows, halo - half)), axis=0)
    wide = toeplitz(taps, width, 3 * width, width - half)
    turned = jnp.concatenate(
        [wide[:, (2 - k) * width : (3 - k) * width] for k in range(3)], axis=1
    )
    sideways = jnp.concatenate(split(jnp.where(mirror == 0, wide, turned)), axis=0)

    node_count = levels_w * levels_a
    tables = jnp.concatenate([gain_ref[...], path_ref[...], albedo_ref[...]], axis=0)
    spread_a = lax.broadcasted_iota(jnp.int32, (levels_a, node_count), 0)
    spread_n = lax.broadcasted_iota(jnp.int32, (levels_a, node_count), 1)
    spread = jnp.where(spread_n % levels_a == spread_a, 1.0, 0.0).astype(bf16)
    wide = jnp.dot(tables, spread, preferred_element_type=f32)
    wide_w = lax.broadcasted_iota(jnp.int32, wide.shape, 0) % levels_w
    wide_n = lax.broadcasted_iota(jnp.int32, wide.shape, 1) // levels_a
    wide = jnp.where(wide_w == wide_n, wide, 0.0).astype(bf16)
    table_rows = levels_e * bands
    into = lax.broadcasted_iota(jnp.int32, (3 * table_rows, wide.shape[0]), 0)
    source = lax.broadcasted_iota(jnp.int32, (3 * table_rows, wide.shape[0]), 1) // levels_w
    within = into % table_rows
    wanted = into - within + (within % bands) * levels_e + within // bands
    lut = jnp.dot(
        jnp.where(source == wanted, 1.0, 0.0).astype(bf16), wide, preferred_element_type=f32
    ).astype(bf16)

    for load in loads[8:]:
        load.wait()
    for w in range(levels_w):
        weight_w = jnp.maximum(0.0, 1.0 - jnp.abs(vapour_ref[...] - float(w)))
        weights[w] = weight_w.reshape(seg_dev, SEG, cols)
    heights[...] = class_ref[...].astype(f32) + frac_ref[...]

    def wait_piece(piece):
        for index, da in enumerate((-1, 1)):

            @pl.when(exists(along - da, n_along))
            def _():
                halo_copy(index, piece).wait_recv()

    def start_side(index):
        @pl.when(exists((inner, outer)[index], n_across))
        def _():
            side_copy(index).start()

    def wait_side(index):
        @pl.when(exists((inner, outer)[index], n_across))
        def _():
            side_copy(index).wait_recv()

    def fall(tile):
        product = jnp.dot(
            down, padded[:, tile * pair : (tile + 1) * pair], preferred_element_type=f32
        )
        high, low = split(product[:rows] + product[rows:])
        at = slice(tile * width, (tile + 1) * width)
        tall[0:rows, at] = high[:, :width]
        tall[rows : 2 * rows, at] = high[:, width:]
        tall[2 * rows : 3 * rows, at] = low[:, :width]
        tall[3 * rows : 4 * rows, at] = low[:, width:]

    def smooth(chunk):
        fresh = [chunk + 2] if chunk else [1, 2, 0]
        for tile in fresh:
            if tile == 0:
                wait_side(1)
            elif tile == chunks + 1:
                wait_side(0)
            elif (tile - 1) % per_piece == 0:
                wait_piece((tile - 1) // per_piece)
                if tile == 1:
                    start_side(1)
                if tile + per_piece == chunks + 1:
                    start_side(0)
            fall(tile)
        product = dot_nt(tall[:, chunk * width : (chunk + 3) * width], sideways)
        smoothed = product[: 2 * rows, :width] + (
            product[2 * rows :, :width] + product[: 2 * rows, width:]
        )
        aerosol = smoothed[:rows] / jnp.maximum(smoothed[rows:], 1.0)
        pos_ref[...] = (levels_a - 1) * jax.nn.sigmoid(aerosol)

    chosen = []
    for number, side in enumerate(SIDES):
        rank = jnp.int32(0)
        first = [jnp.int32(0) for _ in range(CAP)]
        for s in range(seg_dev):
            hit = routes_ref[1, s] - along == side
            for k in range(CAP):
                first[k] = jnp.where(hit & (rank == k), s, first[k])
            rank = rank + jnp.where(hit, 1, 0)
        chosen.append(first)

    node_a = lax.broadcasted_iota(jnp.int32, (levels_a, width), 0).astype(f32)
    sub = lax.broadcasted_iota(jnp.int32, (8, width), 0)
    lower = sub < bands
    pair_e = (sub // bands).astype(f32)
    per_tile = 8 // bands
    quad = 16 // bands
    group = max(1, 256 // width)

    def correct(chunk, seg):
        at_cols = lanes_of(chunk)
        base = pl.multiple_of(seg * SEG, SEG)
        base_flat = pl.multiple_of(seg * seg_rows, seg_rows)
        position = pos_ref[pl.ds(base, SEG), :]
        height_rows = heights[pl.ds(base, SEG), at_cols]
        for first in range(0, SEG, quad):
            partial = []
            values = []
            for start in range(first, first + quad, group):
                joints = []
                for row in range(start, start + group):
                    weight_a = jnp.maximum(0.0, 1.0 - jnp.abs(position[row : row + 1] - node_a))
                    joints.append(
                        jnp.concatenate(
                            [
                                (weight_a * weights[w, seg, row : row + 1, at_cols]).astype(bf16)
                                for w in range(levels_w)
                            ],
                            axis=0,
                        )
                    )
                joint = joints[0] if group == 1 else jnp.concatenate(joints, axis=1)
                product = jnp.dot(lut, joint, preferred_element_type=f32)
                for k in range(group):
                    values.append(product[:, k * width : (k + 1) * width])
            for row in range(first, first + quad):
                nodes = values[row - first]
                height = height_rows[row : row + 1]
                sums = [None] * 3
                for k in range(table_rows // 8):
                    weight_e = jnp.maximum(
                        0.0, 1.0 - jnp.abs(height - (pair_e + float(per_tile * k)))
                    )
                    for t in range(3):
                        at = t * table_rows + k * 8
                        term = nodes[at : at + 8] * weight_e
                        sums[t] = term if sums[t] is None else sums[t] + term
                partial.append(sums)
            radiance = toa_ref[pl.ds(base_flat + first * bands, quad * bands), at_cols].astype(f32)
            surfaces = []
            for part in range(quad // 2):
                coefficient = []
                for t in range(3):
                    one, two = partial[2 * part][t], partial[2 * part + 1][t]
                    kept = jnp.where(lower, one, two)
                    moved = pltpu.roll(jnp.where(lower, two, one), bands, 0)
                    coefficient.append(kept + moved)
                scaled = coefficient[0] * radiance[part * 8 : part * 8 + 8] - coefficient[1]
                surfaces.append(scaled / (1.0 + coefficient[2] * scaled))
            corrected[chunk, seg, first * bands : (first + quad) * bands, :] = jnp.concatenate(
                surfaces, axis=0
            ).astype(bf16)

    def correct_all(chunk):
        def step(seg, carry):
            correct(chunk, seg)
            return carry

        lax.fori_loop(0, seg_dev, step, 0)

    def fill_slots(chunk):
        for number in range(len(SIDES)):
            for k in range(CAP):
                into = (number * CAP + k) * seg_rows
                slots[chunk, into : into + seg_rows] = corrected[chunk, chosen[number][k]]

    def start_slots(chunk):
        for number in order:

            @pl.when(exists(along + SIDES[number], n_along))
            def _():
                slot_copy(chunk, number).start()

    def placed(target):
        row = lax.broadcasted_iota(jnp.int32, (own_rows, target.shape[1]), 0).astype(f32)
        return jnp.where(row == target, 1.0, 0.0).astype(bf16)

    def make_place():
        lane = lax.broadcasted_iota(jnp.int32, (1, own_rows), 1)
        target = jnp.full((1, own_rows), -1, jnp.int32)
        for s in range(seg_dev):
            inside = (lane >= s * seg_rows) & (lane < (s + 1) * seg_rows)
            inside = inside & (routes_ref[0, s] == along)
            target = jnp.where(inside, starts_ref[0, s] * bands + lane - s * seg_rows, target)
        place[:, 0:own_rows] = placed(target.astype(f32))
        for number in order:

            @pl.when(exists(along - SIDES[number], n_along))
            def _():
                tag_copy(number).wait_recv()

            begin = own_rows + number * CAP * seg_rows
            place[:, begin : begin + CAP * seg_rows] = placed(got_tags[number, 0:1, :])
        ones = jnp.ones((place.shape[1], width), bf16)
        count = jnp.dot(place[...], ones, preferred_element_type=f32)
        scale[...] = jnp.maximum(count, 1.0)

    def put(chunk):
        for number in order:

            @pl.when(exists(along - SIDES[number], n_along))
            def _():
                slot_copy(chunk, number).wait_recv()

        mine = corrected[chunk].reshape(own_rows, width)
        segments = jnp.concatenate([mine, got_rows[chunk]], axis=0)
        summed = jnp.dot(place[...], segments, preferred_element_type=f32)
        result = (summed / scale[...]).reshape(rows, bands, width)
        out_ref[:, :, lanes_of(chunk)] = result.astype(bf16)

    if pieces > 1:
        start_halo(1)
    for chunk in range(chunks):
        smooth(chunk)
        if chunk + 2 < pieces:
            start_halo(chunk + 2)
        if chunk:
            start_slots(chunk - 1)
        correct_all(chunk)
        fill_slots(chunk)
        if chunk == min(chunks - 1, 1):
            make_place()
        if chunk >= LAG:
            put(chunk - LAG)
    start_slots(chunks - 1)
    for chunk in range(max(0, chunks - LAG), chunks):
        put(chunk)

    for index, da in enumerate((-1, 1)):

        @pl.when(exists(along + da, n_along))
        def _():
            for piece in range(pieces):
                halo_copy(index, piece).wait_send()

    for index, peer in enumerate((inner, outer)):

        @pl.when(exists(peer, n_across))
        def _():
            side_copy(index).wait_send()

    for number in order:

        @pl.when(exists(along + SIDES[number], n_along))
        def _():
            tag_copy(number).wait_send()
            for chunk in range(chunks):
                slot_copy(chunk, number).wait_send()


def body(
    n_along,
    n_across,
    toa_bands,
    dark_mask,
    vapour,
    elev_class,
    elev_frac,
    kernel,
    lut_gain,
    lut_path,
    lut_albedo,
    routes,
    starts,
):
    rows, bands, cols = toa_bands.shape
    half = kernel.shape[0] // 2
    halo = -(-half // 16) * 16
    levels = lut_gain.shape[1:]
    levels_e, levels_a, levels_w = levels
    seg_dev = routes.shape[0]
    seg_rows = SEG * bands
    side_count = len(SIDES)
    width = math.gcd(cols, WIDTH)
    chunks = cols // width
    pieces = chunks // math.gcd(chunks, 2)
    vmem = pl.BlockSpec(memory_space=pltpu.VMEM)
    hbm = pl.BlockSpec(memory_space=pltpu.HBM)
    table_shape = (bands * levels_e * levels_w, levels_a)
    dma = pltpu.SemaphoreType.DMA

    def table(lut):
        return lut.transpose(0, 1, 3, 2).reshape(table_shape)

    out = pl.pallas_call(
        functools.partial(main_kernel, n_along, n_across, bands, levels),
        out_shape=jax.ShapeDtypeStruct((rows, bands, cols), bf16),
        in_specs=[hbm] * 11,
        out_specs=vmem,
        scratch_shapes=[
            pltpu.SMEM((2, seg_dev), jnp.int32),
            pltpu.SMEM((2, seg_dev), jnp.int32),
            pltpu.VMEM((rows, bands, cols), bf16),
            pltpu.VMEM((rows, cols), jnp.int32),
            pltpu.VMEM((1, kernel.shape[0]), f32),
            pltpu.VMEM(table_shape, bf16),
            pltpu.VMEM(table_shape, bf16),
            pltpu.VMEM(table_shape, bf16),
            pltpu.VMEM((rows, cols), f32),
            pltpu.VMEM((rows, cols), jnp.int32),
            pltpu.VMEM((rows, cols), f32),
            pltpu.VMEM((rows * bands, cols), bf16),
            pltpu.VMEM((side_count, 8, CAP * seg_rows), f32),
            pltpu.VMEM((8, LANES), f32),
            pltpu.VMEM((rows + 2 * halo, (chunks + 2) * 2 * width), bf16),
            pltpu.VMEM((4 * rows, (chunks + 2) * width), bf16),
            pltpu.VMEM((rows, width), f32),
            pltpu.VMEM((levels_w, seg_dev, SEG, cols), f32),
            pltpu.VMEM((rows, cols), f32),
            pltpu.VMEM((chunks, seg_dev, seg_rows, width), bf16),
            pltpu.VMEM((chunks, side_count * CAP * seg_rows, width), bf16),
            pltpu.VMEM((chunks, side_count * CAP * seg_rows, width), bf16),
            pltpu.VMEM((side_count, 8, CAP * seg_rows), f32),
            pltpu.VMEM((rows * bands, rows * bands + side_count * CAP * seg_rows), bf16),
            pltpu.VMEM((rows * bands, width), f32),
            dma((11,)),
            dma((2, pieces)),
            dma((2, pieces)),
            dma((2,)),
            dma((2,)),
            dma((side_count,)),
            dma((side_count,)),
            dma((chunks, side_count)),
            dma((chunks, side_count)),
        ],
        compiler_params=pltpu.CompilerParams(
            collective_id=0, has_side_effects=True, vmem_limit_bytes=28 * 1024 * 1024
        ),
        name="main",
    )(
        *(
            pltpu.with_memory_space_constraint(value, pltpu.HBM)
            for value in (
                routes.T,
                starts.T,
                toa_bands,
                dark_mask,
                kernel[None],
                table(lut_gain),
                table(lut_path),
                table(lut_albedo),
                vapour,
                elev_class,
                elev_frac,
            )
        ),
    )
    return out[None]


def solution(mesh):
    in_specs = (
        P(("groups", "along"), None, "across"),
        P(("groups", "along"), "across"),
        P(("groups", "along"), "across"),
        P(("groups", "along"), "across"),
        P(("groups", "along"), "across"),
        P(),
        P(),
        P(),
        P(),
        P(("groups", "along"), None),
        P(("groups", "along"), None),
    )
    out_specs = P(("groups", "along"), None, None, "across")
    run = functools.partial(body, mesh.shape["along"], mesh.shape["across"])
    return jax.shard_map(run, mesh=mesh, in_specs=in_specs, out_specs=out_specs, check_vma=False)
```

```python
import functools
import math

import jax
import jax.numpy as jnp
from jax import lax
from jax.experimental import pallas as pl
from jax.experimental.pallas import tpu as pltpu
from jax.sharding import PartitionSpec as P

SEG = 16
REACH = 2
CAP = 2
LANES = 128
WIDTH = 128
MESH_ID = pl.DeviceIdType.MESH
SIDES = [side - REACH for side in range(REACH)] + [side + 1 for side in range(REACH)]
LAG = 8
EARLY = 5
f32 = jnp.float32
bf16 = jnp.bfloat16


def split(value):
    high = value.astype(bf16)
    return high, (value - high.astype(f32)).astype(bf16)


def toeplitz(taps, row_count, width, first):
    line = jnp.broadcast_to(taps, (8, taps.shape[1]))
    if width > taps.shape[1]:
        line = jnp.concatenate([line, jnp.zeros((8, width - taps.shape[1]), f32)], axis=1)
    stair = pltpu.roll(line, 0, 1, stride=1, stride_axis=0)
    return jnp.concatenate(
        [pltpu.roll(stair, first + 8 * group, 1) for group in range(row_count // 8)], axis=0
    )


def dot_nt(left, right):
    return lax.dot_general(left, right, (((1,), (1,)), ((), ())), preferred_element_type=f32)


def exists(position, count):
    return (position >= 0) & (position < count)


def main_kernel(
    n_along,
    n_across,
    bands,
    levels,
    routes_hbm,
    starts_hbm,
    toa_hbm,
    mask_hbm,
    taps_hbm,
    gain_hbm,
    path_hbm,
    albedo_hbm,
    vapour_hbm,
    class_hbm,
    frac_hbm,
    out_ref,
    routes_ref,
    starts_ref,
    raw_ref,
    mask_ref,
    taps_ref,
    gain_ref,
    path_ref,
    albedo_ref,
    vapour_ref,
    class_ref,
    frac_ref,
    toa_ref,
    tags_ref,
    taps_pad,
    padded,
    tall,
    pos_ref,
    weights,
    heights,
    corrected,
    slots,
    got_rows,
    got_tags,
    place,
    scale,
    load_sem,
    halo_send,
    halo_recv,
    side_send,
    side_recv,
    tag_send,
    tag_recv,
    slot_send,
    slot_recv,
):
    along, across = lax.axis_index("along"), lax.axis_index("across")
    levels_e, levels_a, levels_w = levels
    rows, _, cols = toa_hbm.shape
    halo = (padded.shape[0] - rows) // 2
    half = taps_hbm.shape[1] // 2
    width = slots.shape[2]
    chunks = cols // width
    seg_rows = SEG * bands
    seg_dev = rows // SEG
    own_rows = rows * bands
    pair = 2 * width
    mirror = across % 2
    inner = across + 1 - 2 * mirror
    outer = across - 1 + 2 * mirror
    pieces = halo_recv.shape[1]
    per_piece = chunks // pieces

    def lanes_of(chunk):
        at = jnp.where(mirror == 0, chunk, chunks - 1 - chunk) * width
        return pl.ds(pl.multiple_of(at, width), width)

    loads = [
        pltpu.make_async_copy(source, target, load_sem.at[number if number < 4 else number - 4])
        for number, (source, target) in enumerate(
            (
                (routes_hbm, routes_ref),
                (starts_hbm, starts_ref),
                (toa_hbm, raw_ref),
                (mask_hbm, mask_ref),
                (taps_hbm, taps_ref),
                (gain_hbm, gain_ref),
                (path_hbm, path_ref),
                (albedo_hbm, albedo_ref),
                (vapour_hbm, vapour_ref),
                (class_hbm, class_ref),
                (frac_hbm, frac_ref),
            )
        )
    ]
    for load in loads[:4]:
        load.start()
    barrier = pltpu.get_barrier_semaphore()
    peers = [
        (exists(along + da, n_along), {"along": along + da})
        for da in sorted({-1, 1, *SIDES}, key=abs)
    ]
    peers += [
        (exists(inner, n_across), {"across": inner}),
        (exists(outer, n_across), {"across": outer}),
    ]
    for present, peer in peers:

        @pl.when(present)
        def _():
            pl.semaphore_signal(barrier, inc=1, device_id=peer, device_id_type=MESH_ID)

    row = lax.broadcasted_iota(jnp.int32, (rows, rows * bands), 0) * bands
    col = lax.broadcasted_iota(jnp.int32, (rows, rows * bands), 1)
    pick = jnp.where(col == row, 8.0, 0.0) + jnp.where(col == row + 2, -4.0, 0.0)
    for load in loads[:4]:
        load.wait()
    for load in loads[4:]:
        load.start()
    flat = raw_ref[...].astype(f32).reshape(rows * bands, cols).astype(bf16)
    toa_ref[...] = flat
    value = jnp.dot(pick.astype(bf16), flat, preferred_element_type=f32)
    darkness = mask_ref[...].astype(f32)
    weighted = (darkness * value).astype(bf16)
    darkness = darkness.astype(bf16)
    for tile in range(chunks):
        own = slice(tile * width, (tile + 1) * width)
        at = pl.multiple_of((jnp.where(mirror == 0, tile, chunks - 1 - tile) + 1) * pair, pair)
        padded[halo : halo + rows, pl.ds(at, width)] = weighted[:, own]
        padded[halo : halo + rows, pl.ds(at + width, width)] = darkness[:, own]

    lane = lax.broadcasted_iota(jnp.int32, (8, CAP * seg_rows), 1)
    for number, side in enumerate(SIDES):
        target = jnp.full((8, CAP * seg_rows), -1, jnp.int32)
        rank = jnp.int32(0)
        for s in range(seg_dev):
            hit = routes_ref[1, s] - along == side
            spot = jnp.where(hit, rank, -1)
            inside = (lane >= spot * seg_rows) & (lane < (spot + 1) * seg_rows) & (spot >= 0)
            target = jnp.where(inside, starts_ref[1, s] * bands + lane - spot * seg_rows, target)
            rank = rank + jnp.where(hit, 1, 0)
        tags_ref[number] = target.astype(f32)

    spans = {
        -1: (slice(halo, 2 * halo), slice(halo + rows, 2 * halo + rows)),
        1: (slice(rows, halo + rows), slice(0, halo)),
    }

    def halo_copy(index, piece):
        da = (-1, 1)[index]
        begin = (1 + piece * per_piece) * pair
        at = slice(begin, begin + per_piece * pair)
        return pltpu.make_async_remote_copy(
            src_ref=padded.at[spans[da][0], at],
            dst_ref=padded.at[spans[da][1], at],
            send_sem=halo_send.at[index],
            recv_sem=halo_recv.at[index, piece],
            device_id={"along": along + da},
            device_id_type=MESH_ID,
        )

    def halo_whole(index):
        da = (-1, 1)[index]
        at = slice(pair, (1 + chunks) * pair)
        return pltpu.make_async_remote_copy(
            src_ref=padded.at[spans[da][0], at],
            dst_ref=padded.at[spans[da][1], at],
            send_sem=halo_send.at[index],
            recv_sem=halo_recv.at[index, 0],
            device_id={"along": along + da},
            device_id_type=MESH_ID,
        )

    def side_copy(index):
        source, target = ((chunks, chunks + 1), (1, 0))[index]
        return pltpu.make_async_remote_copy(
            src_ref=padded.at[:, source * pair : (source + 1) * pair],
            dst_ref=padded.at[:, target * pair : (target + 1) * pair],
            send_sem=side_send.at[index],
            recv_sem=side_recv.at[index],
            device_id={"across": (inner, outer)[index]},
            device_id_type=MESH_ID,
        )

    def tag_copy(number):
        return pltpu.make_async_remote_copy(
            src_ref=tags_ref.at[number],
            dst_ref=got_tags.at[number],
            send_sem=tag_send,
            recv_sem=tag_recv,
            device_id={"along": along + SIDES[number]},
            device_id_type=MESH_ID,
        )

    def slot_copy(chunk, number):
        count = CAP * seg_rows
        return pltpu.make_async_remote_copy(
            src_ref=slots.at[chunk, number * count : (number + 1) * count],
            dst_ref=got_rows.at[chunk, number * count : (number + 1) * count],
            send_sem=slot_send,
            recv_sem=slot_recv.at[chunk],
            device_id={"along": along + SIDES[number]},
            device_id_type=MESH_ID,
        )

    def count_of(flags):
        return sum(flag.astype(jnp.int32) for flag in flags)

    half_count = len(SIDES) // 2
    gone = [exists(along + side, n_along) for side in SIDES]
    come = [exists(along - side, n_along) for side in SIDES]
    gone_first = half_count - count_of(gone[:half_count])
    come_first = half_count - count_of(come[:half_count])
    gone_count, come_count = count_of(gone), count_of(come)
    per_side = CAP * seg_rows

    def tags_wait(first, count, sent):
        for k in range(1, len(SIDES) + 1):

            @pl.when(count == k)
            def _():
                copy = pltpu.make_async_remote_copy(
                    src_ref=tags_ref.at[pl.ds(first, k)],
                    dst_ref=got_tags.at[pl.ds(first, k)],
                    send_sem=tag_send,
                    recv_sem=tag_recv,
                    device_id={"along": along},
                    device_id_type=MESH_ID,
                )
                if sent:
                    copy.wait_send()
                else:
                    copy.wait_recv()

    def slots_wait(first, count, chunk):
        for k in range(1, len(SIDES) + 1):

            @pl.when(count == k)
            def _():
                at = pl.ds(pl.multiple_of(first * per_side, per_side), k * per_side)
                which = slice(0, chunks) if chunk is None else chunk
                copy = pltpu.make_async_remote_copy(
                    src_ref=slots.at[which, at],
                    dst_ref=got_rows.at[which, at],
                    send_sem=slot_send,
                    recv_sem=slot_recv.at[0 if chunk is None else chunk],
                    device_id={"along": along},
                    device_id_type=MESH_ID,
                )
                if chunk is None:
                    copy.wait_send()
                else:
                    copy.wait_recv()

    def start_halo(piece):
        for index, da in enumerate((-1, 1)):

            @pl.when(exists(along + da, n_along))
            def _():
                halo_copy(index, piece).start()

    pl.semaphore_wait(barrier, sum(present.astype(jnp.int32) for present, _ in peers))
    start_halo(0)
    order = sorted(range(len(SIDES)), key=lambda number: abs(SIDES[number]))
    for number in order:

        @pl.when(exists(along + SIDES[number], n_along))
        def _():
            tag_copy(number).start()

        @pl.when(jnp.logical_not(exists(along - SIDES[number], n_along)))
        def _():
            begin = number * CAP * seg_rows
            got_rows[:, begin : begin + CAP * seg_rows, :] = jnp.zeros(
                (chunks, CAP * seg_rows, width), bf16
            )
            got_tags[number] = jnp.full(got_tags.shape[1:], -1.0, f32)

    for da in (-1, 1):

        @pl.when(jnp.logical_not(exists(along - da, n_along)))
        def _():
            padded[spans[da][1], pair : (chunks + 1) * pair] = jnp.zeros(
                (halo, chunks * pair), bf16
            )

    for index, (peer, target) in enumerate(((inner, chunks + 1), (outer, 0))):

        @pl.when(jnp.logical_not(exists(peer, n_across)))
        def _():
            padded[:, target * pair : (target + 1) * pair] = jnp.zeros(
                (padded.shape[0], pair), bf16
            )

    for load in loads[4:8]:
        load.wait()
    taps_pad[...] = jnp.zeros(taps_pad.shape, f32)
    taps_pad[0:1, 0 : taps_ref.shape[1]] = taps_ref[...]
    taps = taps_pad[0:1, :]
    down = jnp.concatenate(split(toeplitz(taps, rows, 2 * halo + rows, halo - half)), axis=0)
    wide = toeplitz(taps, width, 3 * width, width - half)
    turned = jnp.concatenate(
        [wide[:, (2 - k) * width : (3 - k) * width] for k in range(3)], axis=1
    )
    sideways = jnp.concatenate(split(jnp.where(mirror == 0, wide, turned)), axis=0)

    node_count = levels_w * levels_a
    tables = jnp.concatenate([gain_ref[...], path_ref[...], albedo_ref[...]], axis=0)
    spread_a = lax.broadcasted_iota(jnp.int32, (levels_a, node_count), 0)
    spread_n = lax.broadcasted_iota(jnp.int32, (levels_a, node_count), 1)
    spread = jnp.where(spread_n % levels_a == spread_a, 1.0, 0.0).astype(bf16)
    wide = jnp.dot(tables, spread, preferred_element_type=f32)
    wide_w = lax.broadcasted_iota(jnp.int32, wide.shape, 0) % levels_w
    wide_n = lax.broadcasted_iota(jnp.int32, wide.shape, 1) // levels_a
    wide = jnp.where(wide_w == wide_n, wide, 0.0).astype(bf16)
    table_rows = levels_e * bands
    into = lax.broadcasted_iota(jnp.int32, (3 * table_rows, wide.shape[0]), 0)
    source = lax.broadcasted_iota(jnp.int32, (3 * table_rows, wide.shape[0]), 1) // levels_w
    within = into % table_rows
    wanted = into - within + (within % bands) * levels_e + within // bands
    lut = jnp.dot(
        jnp.where(source == wanted, 1.0, 0.0).astype(bf16), wide, preferred_element_type=f32
    ).astype(bf16)

    for load in loads[8:]:
        load.wait()
    sub = lax.broadcasted_iota(jnp.int32, (8, width), 0)
    lower = sub < bands
    pair_e = (sub // bands).astype(f32)
    per_tile = 8 // bands

    def prepare(index, carry):
        at_cols = pl.ds(pl.multiple_of((index // seg_dev) * width, width), width)
        base = pl.multiple_of((index % seg_dev) * SEG, SEG)
        at_rows = pl.ds(base, SEG)
        vapour = vapour_ref[at_rows, at_cols]
        height = class_ref[at_rows, at_cols].astype(f32) + frac_ref[at_rows, at_cols]
        for w in range(levels_w):
            weights[w, index % seg_dev, :, at_cols] = jnp.maximum(0.0, 1.0 - jnp.abs(vapour - float(w)))
        for row in range(SEG):
            for k in range(table_rows // 8):
                heights[base + row, k, :, at_cols] = jnp.maximum(
                    0.0, 1.0 - jnp.abs(height[row : row + 1] - (pair_e + float(per_tile * k)))
                )
        return carry

    early = seg_dev * chunks * EARLY // 16
    lax.fori_loop(0, early, prepare, 0)
    if pieces > 1:
        start_halo(1)
    lax.fori_loop(early, seg_dev * chunks, prepare, 0)
    if pieces > 2:
        start_halo(2)

    def wait_piece(piece):
        for index, da in enumerate((-1, 1)):

            @pl.when(exists(along - da, n_along))
            def _():
                halo_copy(index, piece).wait_recv()

    def start_side(index):
        @pl.when(exists((inner, outer)[index], n_across))
        def _():
            side_copy(index).start()

    def wait_side(index):
        @pl.when(exists((inner, outer)[index], n_across))
        def _():
            side_copy(index).wait_recv()

    def fall(tile):
        product = jnp.dot(
            down, padded[:, tile * pair : (tile + 1) * pair], preferred_element_type=f32
        )
        high, low = split(product[:rows] + product[rows:])
        at = slice(tile * width, (tile + 1) * width)
        tall[0:rows, at] = high[:, :width]
        tall[rows : 2 * rows, at] = high[:, width:]
        tall[2 * rows : 3 * rows, at] = low[:, :width]
        tall[3 * rows : 4 * rows, at] = low[:, width:]

    def smooth(chunk):
        fresh = [chunk + 2] if chunk else [1, 2, 0]
        for tile in fresh:
            if tile == 0:
                wait_side(1)
            elif tile == chunks + 1:
                wait_side(0)
            elif (tile - 1) % per_piece == 0:
                wait_piece((tile - 1) // per_piece)
                if tile == 1:
                    start_side(1)
                if tile + per_piece == chunks + 1:
                    start_side(0)
            fall(tile)
        product = dot_nt(tall[:, chunk * width : (chunk + 3) * width], sideways)
        smoothed = product[: 2 * rows, :width] + (
            product[2 * rows :, :width] + product[: 2 * rows, width:]
        )
        aerosol = smoothed[:rows] / jnp.maximum(smoothed[rows:], 1.0)
        pos_ref[...] = (levels_a - 1) * jax.nn.sigmoid(aerosol)

    chosen = []
    for number, side in enumerate(SIDES):
        rank = jnp.int32(0)
        first = [jnp.int32(0) for _ in range(CAP)]
        for s in range(seg_dev):
            hit = routes_ref[1, s] - along == side
            for k in range(CAP):
                first[k] = jnp.where(hit & (rank == k), s, first[k])
            rank = rank + jnp.where(hit, 1, 0)
        chosen.append(first)

    node_a = lax.broadcasted_iota(jnp.int32, (levels_a, width), 0).astype(f32)
    quad = 16 // bands
    group = max(1, 256 // width)

    def correct(chunk, seg):
        at_cols = lanes_of(chunk)
        base = pl.multiple_of(seg * SEG, SEG)
        base_flat = pl.multiple_of(seg * seg_rows, seg_rows)
        position = pos_ref[pl.ds(base, SEG), :]
        for first in range(0, SEG, quad):
            partial = []
            values = []
            for start in range(first, first + quad, group):
                joints = []
                for row in range(start, start + group):
                    weight_a = jnp.maximum(0.0, 1.0 - jnp.abs(position[row : row + 1] - node_a))
                    weight_a = weight_a.astype(bf16)
                    joints.append(
                        jnp.concatenate(
                            [
                                weight_a
                                * jnp.broadcast_to(
                                    weights[w, seg, row : row + 1, at_cols], (levels_a, width)
                                ).astype(bf16)
                                for w in range(levels_w)
                            ],
                            axis=0,
                        )
                    )
                joint = joints[0] if group == 1 else jnp.concatenate(joints, axis=1)
                product = jnp.dot(lut, joint, preferred_element_type=f32)
                for k in range(group):
                    values.append(product[:, k * width : (k + 1) * width])
            for row in range(first, first + quad):
                nodes = values[row - first]
                sums = [None] * 3
                for k in range(table_rows // 8):
                    weight_e = heights[base + row, k, :, at_cols]
                    for t in range(3):
                        at = t * table_rows + k * 8
                        term = nodes[at : at + 8] * weight_e
                        sums[t] = term if sums[t] is None else sums[t] + term
                partial.append(sums)
            radiance = toa_ref[pl.ds(base_flat + first * bands, quad * bands), at_cols].astype(f32)
            surfaces = []
            for part in range(quad // 2):
                coefficient = []
                for t in range(3):
                    one, two = partial[2 * part][t], partial[2 * part + 1][t]
                    kept = jnp.where(lower, one, two)
                    moved = pltpu.roll(jnp.where(lower, two, one), bands, 0)
                    coefficient.append(kept + moved)
                scaled = coefficient[0] * radiance[part * 8 : part * 8 + 8] - coefficient[1]
                surfaces.append(scaled / (1.0 + coefficient[2] * scaled))
            corrected[chunk, seg, first * bands : (first + quad) * bands, :] = jnp.concatenate(
                surfaces, axis=0
            ).astype(bf16)

    def correct_all(chunk):
        def step(seg, carry):
            correct(chunk, seg)
            return carry

        lax.fori_loop(0, seg_dev, step, 0, unroll=True)

    def fill_slots(chunk):
        for number in range(len(SIDES)):
            for k in range(CAP):
                into = (number * CAP + k) * seg_rows
                slots[chunk, into : into + seg_rows] = corrected[chunk, chosen[number][k]]

    def start_slots(chunk):
        for number in order:

            @pl.when(exists(along + SIDES[number], n_along))
            def _():
                slot_copy(chunk, number).start()

    def placed(target):
        row = lax.broadcasted_iota(jnp.int32, (own_rows, target.shape[1]), 0).astype(f32)
        return jnp.where(row == target, 1.0, 0.0).astype(bf16)

    def make_place():
        lane = lax.broadcasted_iota(jnp.int32, (1, own_rows), 1)
        target = jnp.full((1, own_rows), -1, jnp.int32)
        for s in range(seg_dev):
            inside = (lane >= s * seg_rows) & (lane < (s + 1) * seg_rows)
            inside = inside & (routes_ref[0, s] == along)
            target = jnp.where(inside, starts_ref[0, s] * bands + lane - s * seg_rows, target)
        place[:, 0:own_rows] = placed(target.astype(f32))
        tags_wait(come_first, come_count, False)
        for number in order:
            begin = own_rows + number * CAP * seg_rows
            place[:, begin : begin + CAP * seg_rows] = placed(got_tags[number, 0:1, :])
        ones = jnp.ones((place.shape[1], width), bf16)
        count = jnp.dot(place[...], ones, preferred_element_type=f32)
        scale[...] = jnp.maximum(count, 1.0)

    def put(chunk):
        slots_wait(come_first, come_count, chunk)
        mine = corrected[chunk].reshape(own_rows, width)
        segments = jnp.concatenate([mine, got_rows[chunk]], axis=0)
        summed = jnp.dot(place[...], segments, preferred_element_type=f32)
        result = (summed / scale[...]).reshape(rows, bands, width)
        out_ref[:, :, lanes_of(chunk)] = result.astype(bf16)

    for chunk in range(chunks):
        smooth(chunk)
        if chunk == 0:
            for piece in range(3, pieces):
                start_halo(piece)
        if chunk > 1:
            start_slots(chunk - 1)
        correct_all(chunk)
        fill_slots(chunk)
        if chunk == 0:
            make_place()
            if chunks > 1:
                start_slots(0)
        if chunk >= LAG:
            put(chunk - LAG)
    start_slots(chunks - 1)
    for chunk in range(max(0, chunks - LAG), chunks):
        put(chunk)

    for index, da in enumerate((-1, 1)):

        @pl.when(exists(along + da, n_along))
        def _():
            halo_whole(index).wait_send()

    for index, peer in enumerate((inner, outer)):

        @pl.when(exists(peer, n_across))
        def _():
            side_copy(index).wait_send()

    tags_wait(gone_first, gone_count, True)
    slots_wait(gone_first, gone_count, None)


def body(
    n_along,
    n_across,
    toa_bands,
    dark_mask,
    vapour,
    elev_class,
    elev_frac,
    kernel,
    lut_gain,
    lut_path,
    lut_albedo,
    routes,
    starts,
):
    rows, bands, cols = toa_bands.shape
    half = kernel.shape[0] // 2
    halo = -(-half // 16) * 16
    levels = lut_gain.shape[1:]
    levels_e, levels_a, levels_w = levels
    seg_dev = routes.shape[0]
    seg_rows = SEG * bands
    side_count = len(SIDES)
    width = math.gcd(cols, WIDTH)
    chunks = cols // width
    pieces = chunks // math.gcd(chunks, 2)
    vmem = pl.BlockSpec(memory_space=pltpu.VMEM)
    hbm = pl.BlockSpec(memory_space=pltpu.HBM)
    table_shape = (bands * levels_e * levels_w, levels_a)
    dma = pltpu.SemaphoreType.DMA

    def table(lut):
        return lut.transpose(0, 1, 3, 2).reshape(table_shape)

    out = pl.pallas_call(
        functools.partial(main_kernel, n_along, n_across, bands, levels),
        out_shape=jax.ShapeDtypeStruct((rows, bands, cols), bf16),
        in_specs=[hbm] * 11,
        out_specs=vmem,
        scratch_shapes=[
            pltpu.SMEM((2, seg_dev), jnp.int32),
            pltpu.SMEM((2, seg_dev), jnp.int32),
            pltpu.VMEM((rows, bands, cols), bf16),
            pltpu.VMEM((rows, cols), jnp.int32),
            pltpu.VMEM((1, kernel.shape[0]), f32),
            pltpu.VMEM(table_shape, bf16),
            pltpu.VMEM(table_shape, bf16),
            pltpu.VMEM(table_shape, bf16),
            pltpu.VMEM((rows, cols), f32),
            pltpu.VMEM((rows, cols), jnp.int32),
            pltpu.VMEM((rows, cols), f32),
            pltpu.VMEM((rows * bands, cols), bf16),
            pltpu.VMEM((side_count, 8, CAP * seg_rows), f32),
            pltpu.VMEM((8, LANES), f32),
            pltpu.VMEM((rows + 2 * halo, (chunks + 2) * 2 * width), bf16),
            pltpu.VMEM((4 * rows, (chunks + 2) * width), bf16),
            pltpu.VMEM((rows, width), f32),
            pltpu.VMEM((levels_w, seg_dev, SEG, cols), f32),
            pltpu.VMEM((rows, levels_e * bands // 8, 8, cols), f32),
            pltpu.VMEM((chunks, seg_dev, seg_rows, width), bf16),
            pltpu.VMEM((chunks, side_count * CAP * seg_rows, width), bf16),
            pltpu.VMEM((chunks, side_count * CAP * seg_rows, width), bf16),
            pltpu.VMEM((side_count, 8, CAP * seg_rows), f32),
            pltpu.VMEM((rows * bands, rows * bands + side_count * CAP * seg_rows), bf16),
            pltpu.VMEM((rows * bands, width), f32),
            dma((7,)),
            dma((2,)),
            dma((2, pieces)),
            dma((2,)),
            dma((2,)),
            dma,
            dma,
            dma,
            dma((chunks,)),
        ],
        compiler_params=pltpu.CompilerParams(
            collective_id=0, has_side_effects=True, vmem_limit_bytes=52 * 1024 * 1024
        ),
        name="main",
    )(
        *(
            pltpu.with_memory_space_constraint(value, pltpu.HBM)
            for value in (
                routes.T,
                starts.T,
                toa_bands,
                dark_mask,
                kernel[None],
                table(lut_gain),
                table(lut_path),
                table(lut_albedo),
                vapour,
                elev_class,
                elev_frac,
            )
        ),
    )
    return out[None]


def solution(mesh):
    in_specs = (
        P(("groups", "along"), None, "across"),
        P(("groups", "along"), "across"),
        P(("groups", "along"), "across"),
        P(("groups", "along"), "across"),
        P(("groups", "along"), "across"),
        P(),
        P(),
        P(),
        P(),
        P(("groups", "along"), None),
        P(("groups", "along"), None),
    )
    out_specs = P(("groups", "along"), None, None, "across")
    run = functools.partial(body, mesh.shape["along"], mesh.shape["across"])
    return jax.shard_map(run, mesh=mesh, in_specs=in_specs, out_specs=out_specs, check_vma=False)
```

```python
import functools
import math

import jax
import jax.numpy as jnp
from jax import lax
from jax.experimental import pallas as pl
from jax.experimental.pallas import tpu as pltpu
from jax.sharding import PartitionSpec as P

SEG = 16
REACH = 2
CAP = 2
LANES = 128
WIDTH = 128
MESH_ID = pl.DeviceIdType.MESH
SIDES = [side - REACH for side in range(REACH)] + [side + 1 for side in range(REACH)]
EARLY = 5
f32 = jnp.float32
bf16 = jnp.bfloat16


def split(value):
    high = value.astype(bf16)
    return high, (value - high.astype(f32)).astype(bf16)


def toeplitz(taps, row_count, width, first):
    line = jnp.broadcast_to(taps, (8, taps.shape[1]))
    if width > taps.shape[1]:
        line = jnp.concatenate([line, jnp.zeros((8, width - taps.shape[1]), f32)], axis=1)
    stair = pltpu.roll(line, 0, 1, stride=1, stride_axis=0)
    return jnp.concatenate(
        [pltpu.roll(stair, first + 8 * group, 1) for group in range(row_count // 8)], axis=0
    )


def dot_nt(left, right):
    return lax.dot_general(left, right, (((1,), (1,)), ((), ())), preferred_element_type=f32)


def exists(position, count):
    return (position >= 0) & (position < count)


def main_kernel(
    n_along,
    n_across,
    bands,
    levels,
    routes_hbm,
    starts_hbm,
    toa_hbm,
    mask_hbm,
    taps_hbm,
    gain_hbm,
    path_hbm,
    albedo_hbm,
    vapour_hbm,
    class_hbm,
    frac_hbm,
    out_ref,
    routes_ref,
    starts_ref,
    raw_ref,
    mask_ref,
    taps_ref,
    gain_ref,
    path_ref,
    albedo_ref,
    vapour_ref,
    class_ref,
    frac_ref,
    toa_ref,
    tags_ref,
    taps_pad,
    padded,
    tall,
    pos_ref,
    weights,
    heights,
    corrected,
    slots,
    got_rows,
    got_tags,
    place,
    scale,
    load_sem,
    halo_send,
    halo_recv,
    side_send,
    side_recv,
    tag_send,
    tag_recv,
    slot_send,
    slot_recv,
):
    along, across = lax.axis_index("along"), lax.axis_index("across")
    levels_e, levels_a, levels_w = levels
    rows, _, cols = toa_hbm.shape
    halo = (padded.shape[0] - rows) // 2
    half = taps_hbm.shape[1] // 2
    width = slots.shape[2]
    chunks = cols // width
    seg_rows = SEG * bands
    seg_dev = rows // SEG
    own_rows = rows * bands
    pair = 2 * width
    mirror = across % 2
    inner = across + 1 - 2 * mirror
    outer = across - 1 + 2 * mirror
    pieces = halo_recv.shape[1]
    per_piece = chunks // pieces

    def lanes_of(chunk):
        at = jnp.where(mirror == 0, chunk, chunks - 1 - chunk) * width
        return pl.ds(pl.multiple_of(at, width), width)

    loads = [
        pltpu.make_async_copy(source, target, load_sem.at[number if number < 4 else number - 4])
        for number, (source, target) in enumerate(
            (
                (routes_hbm, routes_ref),
                (starts_hbm, starts_ref),
                (toa_hbm, raw_ref),
                (mask_hbm, mask_ref),
                (taps_hbm, taps_ref),
                (gain_hbm, gain_ref),
                (path_hbm, path_ref),
                (albedo_hbm, albedo_ref),
                (vapour_hbm, vapour_ref),
                (class_hbm, class_ref),
                (frac_hbm, frac_ref),
            )
        )
    ]
    for load in loads[:4]:
        load.start()
    barrier = pltpu.get_barrier_semaphore()
    peers = [
        (exists(along + da, n_along), {"along": along + da})
        for da in sorted({-1, 1, *SIDES}, key=abs)
    ]
    peers += [
        (exists(inner, n_across), {"across": inner}),
        (exists(outer, n_across), {"across": outer}),
    ]
    for present, peer in peers:

        @pl.when(present)
        def _():
            pl.semaphore_signal(barrier, inc=1, device_id=peer, device_id_type=MESH_ID)

    row = lax.broadcasted_iota(jnp.int32, (rows, rows * bands), 0) * bands
    col = lax.broadcasted_iota(jnp.int32, (rows, rows * bands), 1)
    pick = jnp.where(col == row, 8.0, 0.0) + jnp.where(col == row + 2, -4.0, 0.0)
    for load in loads[:4]:
        load.wait()
    for load in loads[4:]:
        load.start()
    flat = raw_ref[...].astype(f32).reshape(rows * bands, cols).astype(bf16)
    toa_ref[...] = flat
    value = jnp.dot(pick.astype(bf16), flat, preferred_element_type=f32)
    darkness = mask_ref[...].astype(f32)
    weighted = (darkness * value).astype(bf16)
    darkness = darkness.astype(bf16)
    for tile in range(chunks):
        own = slice(tile * width, (tile + 1) * width)
        at = pl.multiple_of((jnp.where(mirror == 0, tile, chunks - 1 - tile) + 1) * pair, pair)
        padded[halo : halo + rows, pl.ds(at, width)] = weighted[:, own]
        padded[halo : halo + rows, pl.ds(at + width, width)] = darkness[:, own]

    lane = lax.broadcasted_iota(jnp.int32, (8, CAP * seg_rows), 1)
    for number, side in enumerate(SIDES):
        target = jnp.full((8, CAP * seg_rows), -1, jnp.int32)
        rank = jnp.int32(0)
        for s in range(seg_dev):
            hit = routes_ref[1, s] - along == side
            spot = jnp.where(hit, rank, -1)
            inside = (lane >= spot * seg_rows) & (lane < (spot + 1) * seg_rows) & (spot >= 0)
            target = jnp.where(inside, starts_ref[1, s] * bands + lane - spot * seg_rows, target)
            rank = rank + jnp.where(hit, 1, 0)
        tags_ref[number] = target.astype(f32)

    spans = {
        -1: (slice(halo, 2 * halo), slice(halo + rows, 2 * halo + rows)),
        1: (slice(rows, halo + rows), slice(0, halo)),
    }

    def halo_copy(index, piece):
        da = (-1, 1)[index]
        begin = (1 + piece * per_piece) * pair
        at = slice(begin, begin + per_piece * pair)
        return pltpu.make_async_remote_copy(
            src_ref=padded.at[spans[da][0], at],
            dst_ref=padded.at[spans[da][1], at],
            send_sem=halo_send.at[index],
            recv_sem=halo_recv.at[index, piece],
            device_id={"along": along + da},
            device_id_type=MESH_ID,
        )

    def halo_whole(index):
        da = (-1, 1)[index]
        at = slice(pair, (1 + chunks) * pair)
        return pltpu.make_async_remote_copy(
            src_ref=padded.at[spans[da][0], at],
            dst_ref=padded.at[spans[da][1], at],
            send_sem=halo_send.at[index],
            recv_sem=halo_recv.at[index, 0],
            device_id={"along": along + da},
            device_id_type=MESH_ID,
        )

    def side_copy(index):
        source, target = ((chunks, chunks + 1), (1, 0))[index]
        return pltpu.make_async_remote_copy(
            src_ref=padded.at[:, source * pair : (source + 1) * pair],
            dst_ref=padded.at[:, target * pair : (target + 1) * pair],
            send_sem=side_send.at[index],
            recv_sem=side_recv.at[index],
            device_id={"across": (inner, outer)[index]},
            device_id_type=MESH_ID,
        )

    def tag_copy(number):
        return pltpu.make_async_remote_copy(
            src_ref=tags_ref.at[number],
            dst_ref=got_tags.at[number],
            send_sem=tag_send,
            recv_sem=tag_recv,
            device_id={"along": along + SIDES[number]},
            device_id_type=MESH_ID,
        )

    def slot_copy(chunk, number):
        count = CAP * seg_rows
        return pltpu.make_async_remote_copy(
            src_ref=slots.at[chunk, number * count : (number + 1) * count],
            dst_ref=got_rows.at[chunk, number * count : (number + 1) * count],
            send_sem=slot_send,
            recv_sem=slot_recv.at[chunk],
            device_id={"along": along + SIDES[number]},
            device_id_type=MESH_ID,
        )

    def count_of(flags):
        return sum(flag.astype(jnp.int32) for flag in flags)

    half_count = len(SIDES) // 2
    gone = [exists(along + side, n_along) for side in SIDES]
    come = [exists(along - side, n_along) for side in SIDES]
    gone_first = half_count - count_of(gone[:half_count])
    come_first = half_count - count_of(come[:half_count])
    gone_count, come_count = count_of(gone), count_of(come)
    per_side = CAP * seg_rows

    def tags_wait(first, count, sent):
        for k in range(1, len(SIDES) + 1):

            @pl.when(count == k)
            def _():
                copy = pltpu.make_async_remote_copy(
                    src_ref=tags_ref.at[pl.ds(first, k)],
                    dst_ref=got_tags.at[pl.ds(first, k)],
                    send_sem=tag_send,
                    recv_sem=tag_recv,
                    device_id={"along": along},
                    device_id_type=MESH_ID,
                )
                if sent:
                    copy.wait_send()
                else:
                    copy.wait_recv()

    def slots_wait(first, count, chunk):
        for k in range(1, len(SIDES) + 1):

            @pl.when(count == k)
            def _():
                at = pl.ds(pl.multiple_of(first * per_side, per_side), k * per_side)
                which = slice(0, chunks) if chunk is None else chunk
                copy = pltpu.make_async_remote_copy(
                    src_ref=slots.at[which, at],
                    dst_ref=got_rows.at[which, at],
                    send_sem=slot_send,
                    recv_sem=slot_recv.at[0 if chunk is None else chunk],
                    device_id={"along": along},
                    device_id_type=MESH_ID,
                )
                if chunk is None:
                    copy.wait_send()
                else:
                    copy.wait_recv()

    def start_halo(piece):
        for index, da in enumerate((-1, 1)):

            @pl.when(exists(along + da, n_along))
            def _():
                halo_copy(index, piece).start()

    pl.semaphore_wait(barrier, sum(present.astype(jnp.int32) for present, _ in peers))
    start_halo(0)
    order = sorted(range(len(SIDES)), key=lambda number: abs(SIDES[number]))
    for number in order:

        @pl.when(exists(along + SIDES[number], n_along))
        def _():
            tag_copy(number).start()

        @pl.when(jnp.logical_not(exists(along - SIDES[number], n_along)))
        def _():
            begin = number * CAP * seg_rows
            got_rows[:, begin : begin + CAP * seg_rows, :] = jnp.zeros(
                (chunks, CAP * seg_rows, width), bf16
            )
            got_tags[number] = jnp.full(got_tags.shape[1:], -1.0, f32)

    for da in (-1, 1):

        @pl.when(jnp.logical_not(exists(along - da, n_along)))
        def _():
            padded[spans[da][1], pair : (chunks + 1) * pair] = jnp.zeros(
                (halo, chunks * pair), bf16
            )

    for index, (peer, target) in enumerate(((inner, chunks + 1), (outer, 0))):

        @pl.when(jnp.logical_not(exists(peer, n_across)))
        def _():
            padded[:, target * pair : (target + 1) * pair] = jnp.zeros(
                (padded.shape[0], pair), bf16
            )

    for load in loads[4:8]:
        load.wait()
    taps_pad[...] = jnp.zeros(taps_pad.shape, f32)
    taps_pad[0:1, 0 : taps_ref.shape[1]] = taps_ref[...]
    taps = taps_pad[0:1, :]
    down = jnp.concatenate(split(toeplitz(taps, rows, 2 * halo + rows, halo - half)), axis=0)
    wide = toeplitz(taps, width, 3 * width, width - half)
    turned = jnp.concatenate(
        [wide[:, (2 - k) * width : (3 - k) * width] for k in range(3)], axis=1
    )
    sideways = jnp.concatenate(split(jnp.where(mirror == 0, wide, turned)), axis=0)

    node_count = levels_w * levels_a
    tables = jnp.concatenate([gain_ref[...], path_ref[...], albedo_ref[...]], axis=0)
    spread_a = lax.broadcasted_iota(jnp.int32, (levels_a, node_count), 0)
    spread_n = lax.broadcasted_iota(jnp.int32, (levels_a, node_count), 1)
    spread = jnp.where(spread_n % levels_a == spread_a, 1.0, 0.0).astype(bf16)
    wide = jnp.dot(tables, spread, preferred_element_type=f32)
    wide_w = lax.broadcasted_iota(jnp.int32, wide.shape, 0) % levels_w
    wide_n = lax.broadcasted_iota(jnp.int32, wide.shape, 1) // levels_a
    wide = jnp.where(wide_w == wide_n, wide, 0.0).astype(bf16)
    table_rows = levels_e * bands
    into = lax.broadcasted_iota(jnp.int32, (3 * table_rows, wide.shape[0]), 0)
    source = lax.broadcasted_iota(jnp.int32, (3 * table_rows, wide.shape[0]), 1) // levels_w
    within = into % table_rows
    wanted = into - within + (within % bands) * levels_e + within // bands
    lut = jnp.dot(
        jnp.where(source == wanted, 1.0, 0.0).astype(bf16), wide, preferred_element_type=f32
    ).astype(bf16)

    for load in loads[8:]:
        load.wait()
    sub = lax.broadcasted_iota(jnp.int32, (8, width), 0)
    lower = sub < bands
    pair_e = (sub // bands).astype(f32)
    per_tile = 8 // bands

    def prepare(index, carry):
        at_cols = pl.ds(pl.multiple_of((index // seg_dev) * width, width), width)
        base = pl.multiple_of((index % seg_dev) * SEG, SEG)
        at_rows = pl.ds(base, SEG)
        vapour = vapour_ref[at_rows, at_cols]
        height = class_ref[at_rows, at_cols].astype(f32) + frac_ref[at_rows, at_cols]
        for w in range(levels_w):
            weights[w, index % seg_dev, :, at_cols] = jnp.maximum(0.0, 1.0 - jnp.abs(vapour - float(w)))
        for row in range(SEG):
            for k in range(table_rows // 8):
                heights[base + row, k, :, at_cols] = jnp.maximum(
                    0.0, 1.0 - jnp.abs(height[row : row + 1] - (pair_e + float(per_tile * k)))
                )
        return carry

    early = seg_dev * chunks * EARLY // 16
    lax.fori_loop(0, early, prepare, 0)
    if pieces > 1:
        start_halo(1)
    lax.fori_loop(early, seg_dev * chunks, prepare, 0)
    if pieces > 2:
        start_halo(2)

    def wait_piece(piece):
        for index, da in enumerate((-1, 1)):

            @pl.when(exists(along - da, n_along))
            def _():
                halo_copy(index, piece).wait_recv()

    def start_side(index):
        @pl.when(exists((inner, outer)[index], n_across))
        def _():
            side_copy(index).start()

    def wait_side(index):
        @pl.when(exists((inner, outer)[index], n_across))
        def _():
            side_copy(index).wait_recv()

    def fall(tile):
        product = jnp.dot(
            down, padded[:, tile * pair : (tile + 1) * pair], preferred_element_type=f32
        )
        high, low = split(product[:rows] + product[rows:])
        at = slice(tile * width, (tile + 1) * width)
        tall[0:rows, at] = high[:, :width]
        tall[rows : 2 * rows, at] = high[:, width:]
        tall[2 * rows : 3 * rows, at] = low[:, :width]
        tall[3 * rows : 4 * rows, at] = low[:, width:]

    def smooth(chunk):
        fresh = [chunk + 2] if chunk else [1, 2, 0]
        for tile in fresh:
            if tile == 0:
                wait_side(1)
            elif tile == chunks + 1:
                wait_side(0)
            elif (tile - 1) % per_piece == 0:
                wait_piece((tile - 1) // per_piece)
                if tile == 1:
                    start_side(1)
                if tile + per_piece == chunks + 1:
                    start_side(0)
            fall(tile)
        product = dot_nt(tall[:, chunk * width : (chunk + 3) * width], sideways)
        smoothed = product[: 2 * rows, :width] + (
            product[2 * rows :, :width] + product[: 2 * rows, width:]
        )
        aerosol = smoothed[:rows] / jnp.maximum(smoothed[rows:], 1.0)
        pos_ref[...] = (levels_a - 1) * jax.nn.sigmoid(aerosol)

    chosen = []
    for number, side in enumerate(SIDES):
        rank = jnp.int32(0)
        first = [jnp.int32(0) for _ in range(CAP)]
        for s in range(seg_dev):
            hit = routes_ref[1, s] - along == side
            for k in range(CAP):
                first[k] = jnp.where(hit & (rank == k), s, first[k])
            rank = rank + jnp.where(hit, 1, 0)
        chosen.append(first)

    node_a = lax.broadcasted_iota(jnp.int32, (levels_a, width), 0).astype(f32)
    quad = 16 // bands
    group = max(1, 256 // width)

    def correct(chunk, seg):
        at_cols = lanes_of(chunk)
        base = pl.multiple_of(seg * SEG, SEG)
        base_flat = pl.multiple_of(seg * seg_rows, seg_rows)
        position = pos_ref[pl.ds(base, SEG), :]
        for first in range(0, SEG, quad):
            partial = []
            values = []
            for start in range(first, first + quad, group):
                joints = []
                for row in range(start, start + group):
                    weight_a = jnp.maximum(0.0, 1.0 - jnp.abs(position[row : row + 1] - node_a))
                    weight_a = weight_a.astype(bf16)
                    joints.append(
                        jnp.concatenate(
                            [
                                weight_a
                                * jnp.broadcast_to(
                                    weights[w, seg, row : row + 1, at_cols], (levels_a, width)
                                ).astype(bf16)
                                for w in range(levels_w)
                            ],
                            axis=0,
                        )
                    )
                joint = joints[0] if group == 1 else jnp.concatenate(joints, axis=1)
                product = jnp.dot(lut, joint, preferred_element_type=f32)
                for k in range(group):
                    values.append(product[:, k * width : (k + 1) * width])
            for row in range(first, first + quad):
                nodes = values[row - first]
                sums = [None] * 3
                for k in range(table_rows // 8):
                    weight_e = heights[base + row, k, :, at_cols]
                    for t in range(3):
                        at = t * table_rows + k * 8
                        term = nodes[at : at + 8] * weight_e
                        sums[t] = term if sums[t] is None else sums[t] + term
                partial.append(sums)
            radiance = toa_ref[pl.ds(base_flat + first * bands, quad * bands), at_cols].astype(f32)
            surfaces = []
            for part in range(quad // 2):
                coefficient = []
                for t in range(3):
                    one, two = partial[2 * part][t], partial[2 * part + 1][t]
                    kept = jnp.where(lower, one, two)
                    moved = pltpu.roll(jnp.where(lower, two, one), bands, 0)
                    coefficient.append(kept + moved)
                scaled = coefficient[0] * radiance[part * 8 : part * 8 + 8] - coefficient[1]
                surfaces.append(scaled / (1.0 + coefficient[2] * scaled))
            corrected[chunk, seg, first * bands : (first + quad) * bands, :] = jnp.concatenate(
                surfaces, axis=0
            ).astype(bf16)

    def correct_all(chunk):
        def step(seg, carry):
            correct(chunk, seg)
            return carry

        lax.fori_loop(0, seg_dev, step, 0, unroll=True)

    def fill_slots(chunk):
        for number in range(len(SIDES)):
            for k in range(CAP):
                into = (number * CAP + k) * seg_rows
                slots[chunk, into : into + seg_rows] = corrected[chunk, chosen[number][k]]

    def start_slot(chunk, number, wanted):
        @pl.when(exists(along + SIDES[number], n_along) & wanted)
        def _():
            slot_copy(chunk, number).start()

    odd = along % 2 == 1
    even = jnp.logical_not(odd)
    near = {number: odd if side < 0 else even for number, side in enumerate(SIDES)}

    def start_slots(chunk):
        for wanted in (0, 1, 2):
            for number, side in enumerate(SIDES):
                if wanted == 1:
                    if abs(side) != 1:
                        start_slot(chunk, number, True)
                elif abs(side) == 1:
                    here = near[number] if wanted == 0 else jnp.logical_not(near[number])
                    start_slot(chunk, number, here)

    def placed(target):
        row = lax.broadcasted_iota(jnp.int32, (own_rows, target.shape[1]), 0).astype(f32)
        return jnp.where(row == target, 1.0, 0.0).astype(bf16)

    def make_place():
        lane = lax.broadcasted_iota(jnp.int32, (1, own_rows), 1)
        target = jnp.full((1, own_rows), -1, jnp.int32)
        for s in range(seg_dev):
            inside = (lane >= s * seg_rows) & (lane < (s + 1) * seg_rows)
            inside = inside & (routes_ref[0, s] == along)
            target = jnp.where(inside, starts_ref[0, s] * bands + lane - s * seg_rows, target)
        place[:, 0:own_rows] = placed(target.astype(f32))
        tags_wait(come_first, come_count, False)
        for number in order:
            begin = own_rows + number * CAP * seg_rows
            place[:, begin : begin + CAP * seg_rows] = placed(got_tags[number, 0:1, :])
        ones = jnp.ones((place.shape[1], width), bf16)
        count = jnp.dot(place[...], ones, preferred_element_type=f32)
        scale[...] = jnp.maximum(count, 1.0)

    def put(first, count):
        for chunk in range(first, first + count):
            slots_wait(come_first, come_count, chunk)
        segments = [
            jnp.concatenate([corrected[chunk].reshape(own_rows, width), got_rows[chunk]], axis=0)
            for chunk in range(first, first + count)
        ]
        segments = segments[0] if count == 1 else jnp.concatenate(segments, axis=1)
        summed = jnp.dot(place[...], segments, preferred_element_type=f32)
        for k in range(count):
            result = summed[:, k * width : (k + 1) * width] / scale[...]
            result = result.reshape(rows, bands, width)
            out_ref[:, :, lanes_of(first + k)] = result.astype(bf16)

    for chunk in range(chunks):
        smooth(chunk)
        if chunk == 0:
            for piece in range(3, pieces):
                start_halo(piece)
        if chunk > 1:
            start_slots(chunk - 1)
        correct_all(chunk)
        fill_slots(chunk)
        if chunk == 0:
            make_place()
            if chunks > 1:
                start_slots(0)
    start_slots(chunks - 1)
    for first in range(0, chunks, 2):
        put(first, min(2, chunks - first))

    for index, da in enumerate((-1, 1)):

        @pl.when(exists(along + da, n_along))
        def _():
            halo_whole(index).wait_send()

    for index, peer in enumerate((inner, outer)):

        @pl.when(exists(peer, n_across))
        def _():
            side_copy(index).wait_send()

    tags_wait(gone_first, gone_count, True)
    slots_wait(gone_first, gone_count, None)


def body(
    n_along,
    n_across,
    toa_bands,
    dark_mask,
    vapour,
    elev_class,
    elev_frac,
    kernel,
    lut_gain,
    lut_path,
    lut_albedo,
    routes,
    starts,
):
    rows, bands, cols = toa_bands.shape
    half = kernel.shape[0] // 2
    halo = -(-half // 16) * 16
    levels = lut_gain.shape[1:]
    levels_e, levels_a, levels_w = levels
    seg_dev = routes.shape[0]
    seg_rows = SEG * bands
    side_count = len(SIDES)
    width = math.gcd(cols, WIDTH)
    chunks = cols // width
    pieces = chunks // math.gcd(chunks, 2)
    vmem = pl.BlockSpec(memory_space=pltpu.VMEM)
    hbm = pl.BlockSpec(memory_space=pltpu.HBM)
    table_shape = (bands * levels_e * levels_w, levels_a)
    dma = pltpu.SemaphoreType.DMA

    def table(lut):
        return lut.transpose(0, 1, 3, 2).reshape(table_shape)

    out = pl.pallas_call(
        functools.partial(main_kernel, n_along, n_across, bands, levels),
        out_shape=jax.ShapeDtypeStruct((rows, bands, cols), bf16),
        in_specs=[hbm] * 11,
        out_specs=vmem,
        scratch_shapes=[
            pltpu.SMEM((2, seg_dev), jnp.int32),
            pltpu.SMEM((2, seg_dev), jnp.int32),
            pltpu.VMEM((rows, bands, cols), bf16),
            pltpu.VMEM((rows, cols), jnp.int32),
            pltpu.VMEM((1, kernel.shape[0]), f32),
            pltpu.VMEM(table_shape, bf16),
            pltpu.VMEM(table_shape, bf16),
            pltpu.VMEM(table_shape, bf16),
            pltpu.VMEM((rows, cols), f32),
            pltpu.VMEM((rows, cols), jnp.int32),
            pltpu.VMEM((rows, cols), f32),
            pltpu.VMEM((rows * bands, cols), bf16),
            pltpu.VMEM((side_count, 8, CAP * seg_rows), f32),
            pltpu.VMEM((8, LANES), f32),
            pltpu.VMEM((rows + 2 * halo, (chunks + 2) * 2 * width), bf16),
            pltpu.VMEM((4 * rows, (chunks + 2) * width), bf16),
            pltpu.VMEM((rows, width), f32),
            pltpu.VMEM((levels_w, seg_dev, SEG, cols), f32),
            pltpu.VMEM((rows, levels_e * bands // 8, 8, cols), f32),
            pltpu.VMEM((chunks, seg_dev, seg_rows, width), bf16),
            pltpu.VMEM((chunks, side_count * CAP * seg_rows, width), bf16),
            pltpu.VMEM((chunks, side_count * CAP * seg_rows, width), bf16),
            pltpu.VMEM((side_count, 8, CAP * seg_rows), f32),
            pltpu.VMEM((rows * bands, rows * bands + side_count * CAP * seg_rows), bf16),
            pltpu.VMEM((rows * bands, width), f32),
            dma((7,)),
            dma((2,)),
            dma((2, pieces)),
            dma((2,)),
            dma((2,)),
            dma,
            dma,
            dma,
            dma((chunks,)),
        ],
        compiler_params=pltpu.CompilerParams(
            collective_id=0, has_side_effects=True, vmem_limit_bytes=52 * 1024 * 1024
        ),
        name="main",
    )(
        *(
            pltpu.with_memory_space_constraint(value, pltpu.HBM)
            for value in (
                routes.T,
                starts.T,
                toa_bands,
                dark_mask,
                kernel[None],
                table(lut_gain),
                table(lut_path),
                table(lut_albedo),
                vapour,
                elev_class,
                elev_frac,
            )
        ),
    )
    return out[None]


def solution(mesh):
    in_specs = (
        P(("groups", "along"), None, "across"),
        P(("groups", "along"), "across"),
        P(("groups", "along"), "across"),
        P(("groups", "along"), "across"),
        P(("groups", "along"), "across"),
        P(),
        P(),
        P(),
        P(),
        P(("groups", "along"), None),
        P(("groups", "along"), None),
    )
    out_specs = P(("groups", "along"), None, None, "across")
    run = functools.partial(body, mesh.shape["along"], mesh.shape["across"])
    return jax.shard_map(run, mesh=mesh, in_specs=in_specs, out_specs=out_specs, check_vma=False)
```

```python
import functools
import math

import jax
import jax.numpy as jnp
from jax import lax
from jax.experimental import pallas as pl
from jax.experimental.pallas import tpu as pltpu
from jax.sharding import PartitionSpec as P

SEG = 16
REACH = 2
CAP = 2
LANES = 128
WIDTH = 128
MESH_ID = pl.DeviceIdType.MESH
SIDES = [side - REACH for side in range(REACH)] + [side + 1 for side in range(REACH)]
EARLY = 5
DEFER = 4
f32 = jnp.float32
bf16 = jnp.bfloat16


def split(value):
    high = value.astype(bf16)
    return high, (value - high.astype(f32)).astype(bf16)


def toeplitz(taps, row_count, width, first):
    line = jnp.broadcast_to(taps, (8, taps.shape[1]))
    if width > taps.shape[1]:
        line = jnp.concatenate([line, jnp.zeros((8, width - taps.shape[1]), f32)], axis=1)
    stair = pltpu.roll(line, 0, 1, stride=1, stride_axis=0)
    return jnp.concatenate(
        [pltpu.roll(stair, first + 8 * group, 1) for group in range(row_count // 8)], axis=0
    )


def dot_nt(left, right):
    return lax.dot_general(left, right, (((1,), (1,)), ((), ())), preferred_element_type=f32)


def averages(place, segments, scale, bands):
    width = scale.shape[1]
    summed = jnp.dot(place, segments, preferred_element_type=f32)
    for k in range(segments.shape[1] // width):
        result = summed[:, k * width : (k + 1) * width] / scale
        yield result.reshape(-1, bands, width).astype(bf16)


def exists(position, count):
    return (position >= 0) & (position < count)


def main_kernel(
    n_along,
    n_across,
    bands,
    levels,
    routes_hbm,
    starts_hbm,
    toa_hbm,
    mask_hbm,
    taps_hbm,
    gain_hbm,
    path_hbm,
    albedo_hbm,
    vapour_hbm,
    class_hbm,
    frac_hbm,
    out_ref,
    rest_ref,
    place,
    scale,
    routes_ref,
    starts_ref,
    raw_ref,
    mask_ref,
    taps_ref,
    gain_ref,
    path_ref,
    albedo_ref,
    vapour_ref,
    class_ref,
    frac_ref,
    toa_ref,
    tags_ref,
    taps_pad,
    padded,
    tall,
    pos_ref,
    weights,
    heights,
    corrected,
    slots,
    got_rows,
    got_tags,
    load_sem,
    halo_send,
    halo_recv,
    side_send,
    side_recv,
    tag_send,
    tag_recv,
    slot_send,
    slot_recv,
):
    along, across = lax.axis_index("along"), lax.axis_index("across")
    levels_e, levels_a, levels_w = levels
    rows, _, cols = toa_hbm.shape
    halo = (padded.shape[0] - rows) // 2
    half = taps_hbm.shape[1] // 2
    width = slots.shape[2]
    chunks = cols // width
    seg_rows = SEG * bands
    seg_dev = rows // SEG
    own_rows = rows * bands
    pair = 2 * width
    mirror = across % 2
    inner = across + 1 - 2 * mirror
    outer = across - 1 + 2 * mirror
    pieces = halo_recv.shape[1]
    per_piece = chunks // pieces

    def lanes_of(chunk):
        at = jnp.where(mirror == 0, chunk, chunks - 1 - chunk) * width
        return pl.ds(pl.multiple_of(at, width), width)

    loads = [
        pltpu.make_async_copy(source, target, load_sem.at[number if number < 4 else number - 4])
        for number, (source, target) in enumerate(
            (
                (routes_hbm, routes_ref),
                (starts_hbm, starts_ref),
                (toa_hbm, raw_ref),
                (mask_hbm, mask_ref),
                (taps_hbm, taps_ref),
                (gain_hbm, gain_ref),
                (path_hbm, path_ref),
                (albedo_hbm, albedo_ref),
                (vapour_hbm, vapour_ref),
                (class_hbm, class_ref),
                (frac_hbm, frac_ref),
            )
        )
    ]
    for load in loads[:4]:
        load.start()
    barrier = pltpu.get_barrier_semaphore()
    peers = [
        (exists(along + da, n_along), {"along": along + da})
        for da in sorted({-1, 1, *SIDES}, key=abs)
    ]
    peers += [
        (exists(inner, n_across), {"across": inner}),
        (exists(outer, n_across), {"across": outer}),
    ]
    for present, peer in peers:

        @pl.when(present)
        def _():
            pl.semaphore_signal(barrier, inc=1, device_id=peer, device_id_type=MESH_ID)

    row = lax.broadcasted_iota(jnp.int32, (rows, rows * bands), 0) * bands
    col = lax.broadcasted_iota(jnp.int32, (rows, rows * bands), 1)
    pick = jnp.where(col == row, 8.0, 0.0) + jnp.where(col == row + 2, -4.0, 0.0)
    for load in loads[:4]:
        load.wait()
    for load in loads[4:]:
        load.start()
    flat = raw_ref[...].astype(f32).reshape(rows * bands, cols).astype(bf16)
    toa_ref[...] = flat
    value = jnp.dot(pick.astype(bf16), flat, preferred_element_type=f32)
    darkness = mask_ref[...].astype(f32)
    weighted = (darkness * value).astype(bf16)
    darkness = darkness.astype(bf16)
    for tile in range(chunks):
        own = slice(tile * width, (tile + 1) * width)
        at = pl.multiple_of((jnp.where(mirror == 0, tile, chunks - 1 - tile) + 1) * pair, pair)
        padded[halo : halo + rows, pl.ds(at, width)] = weighted[:, own]
        padded[halo : halo + rows, pl.ds(at + width, width)] = darkness[:, own]

    lane = lax.broadcasted_iota(jnp.int32, (8, CAP * seg_rows), 1)
    for number, side in enumerate(SIDES):
        target = jnp.full((8, CAP * seg_rows), -1, jnp.int32)
        rank = jnp.int32(0)
        for s in range(seg_dev):
            hit = routes_ref[1, s] - along == side
            spot = jnp.where(hit, rank, -1)
            inside = (lane >= spot * seg_rows) & (lane < (spot + 1) * seg_rows) & (spot >= 0)
            target = jnp.where(inside, starts_ref[1, s] * bands + lane - spot * seg_rows, target)
            rank = rank + jnp.where(hit, 1, 0)
        tags_ref[number] = target.astype(f32)

    spans = {
        -1: (slice(halo, 2 * halo), slice(halo + rows, 2 * halo + rows)),
        1: (slice(rows, halo + rows), slice(0, halo)),
    }

    def halo_copy(index, piece):
        da = (-1, 1)[index]
        begin = (1 + piece * per_piece) * pair
        at = slice(begin, begin + per_piece * pair)
        return pltpu.make_async_remote_copy(
            src_ref=padded.at[spans[da][0], at],
            dst_ref=padded.at[spans[da][1], at],
            send_sem=halo_send.at[index],
            recv_sem=halo_recv.at[index, piece],
            device_id={"along": along + da},
            device_id_type=MESH_ID,
        )

    def halo_whole(index):
        da = (-1, 1)[index]
        at = slice(pair, (1 + chunks) * pair)
        return pltpu.make_async_remote_copy(
            src_ref=padded.at[spans[da][0], at],
            dst_ref=padded.at[spans[da][1], at],
            send_sem=halo_send.at[index],
            recv_sem=halo_recv.at[index, 0],
            device_id={"along": along + da},
            device_id_type=MESH_ID,
        )

    def side_copy(index):
        source, target = ((chunks, chunks + 1), (1, 0))[index]
        return pltpu.make_async_remote_copy(
            src_ref=padded.at[:, source * pair : (source + 1) * pair],
            dst_ref=padded.at[:, target * pair : (target + 1) * pair],
            send_sem=side_send.at[index],
            recv_sem=side_recv.at[index],
            device_id={"across": (inner, outer)[index]},
            device_id_type=MESH_ID,
        )

    def tag_copy(number):
        return pltpu.make_async_remote_copy(
            src_ref=tags_ref.at[number],
            dst_ref=got_tags.at[number],
            send_sem=tag_send,
            recv_sem=tag_recv,
            device_id={"along": along + SIDES[number]},
            device_id_type=MESH_ID,
        )

    def slot_copy(chunk, number):
        count = CAP * seg_rows
        return pltpu.make_async_remote_copy(
            src_ref=slots.at[chunk, number * count : (number + 1) * count],
            dst_ref=got_rows.at[chunk, number * count : (number + 1) * count],
            send_sem=slot_send,
            recv_sem=slot_recv.at[chunk],
            device_id={"along": along + SIDES[number]},
            device_id_type=MESH_ID,
        )

    def count_of(flags):
        return sum(flag.astype(jnp.int32) for flag in flags)

    half_count = len(SIDES) // 2
    gone = [exists(along + side, n_along) for side in SIDES]
    come = [exists(along - side, n_along) for side in SIDES]
    gone_first = half_count - count_of(gone[:half_count])
    come_first = half_count - count_of(come[:half_count])
    gone_count, come_count = count_of(gone), count_of(come)
    per_side = CAP * seg_rows

    def tags_wait(first, count, sent):
        for k in range(1, len(SIDES) + 1):

            @pl.when(count == k)
            def _():
                copy = pltpu.make_async_remote_copy(
                    src_ref=tags_ref.at[pl.ds(first, k)],
                    dst_ref=got_tags.at[pl.ds(first, k)],
                    send_sem=tag_send,
                    recv_sem=tag_recv,
                    device_id={"along": along},
                    device_id_type=MESH_ID,
                )
                if sent:
                    copy.wait_send()
                else:
                    copy.wait_recv()

    def slots_wait(first, count, chunk):
        for k in range(1, len(SIDES) + 1):

            @pl.when(count == k)
            def _():
                at = pl.ds(pl.multiple_of(first * per_side, per_side), k * per_side)
                which = slice(0, chunks) if chunk is None else chunk
                copy = pltpu.make_async_remote_copy(
                    src_ref=slots.at[which, at],
                    dst_ref=got_rows.at[which, at],
                    send_sem=slot_send,
                    recv_sem=slot_recv.at[0 if chunk is None else chunk],
                    device_id={"along": along},
                    device_id_type=MESH_ID,
                )
                if chunk is None:
                    copy.wait_send()
                else:
                    copy.wait_recv()

    def start_halo(piece):
        for index, da in enumerate((-1, 1)):

            @pl.when(exists(along + da, n_along))
            def _():
                halo_copy(index, piece).start()

    pl.semaphore_wait(barrier, sum(present.astype(jnp.int32) for present, _ in peers))
    start_halo(0)
    order = sorted(range(len(SIDES)), key=lambda number: abs(SIDES[number]))
    for number in order:

        @pl.when(exists(along + SIDES[number], n_along))
        def _():
            tag_copy(number).start()

        @pl.when(jnp.logical_not(exists(along - SIDES[number], n_along)))
        def _():
            begin = number * CAP * seg_rows
            got_rows[:, begin : begin + CAP * seg_rows, :] = jnp.zeros(
                (chunks, CAP * seg_rows, width), bf16
            )
            got_tags[number] = jnp.full(got_tags.shape[1:], -1.0, f32)

    for da in (-1, 1):

        @pl.when(jnp.logical_not(exists(along - da, n_along)))
        def _():
            padded[spans[da][1], pair : (chunks + 1) * pair] = jnp.zeros(
                (halo, chunks * pair), bf16
            )

    for index, (peer, target) in enumerate(((inner, chunks + 1), (outer, 0))):

        @pl.when(jnp.logical_not(exists(peer, n_across)))
        def _():
            padded[:, target * pair : (target + 1) * pair] = jnp.zeros(
                (padded.shape[0], pair), bf16
            )

    for load in loads[4:8]:
        load.wait()
    taps_pad[...] = jnp.zeros(taps_pad.shape, f32)
    taps_pad[0:1, 0 : taps_ref.shape[1]] = taps_ref[...]
    taps = taps_pad[0:1, :]
    down = jnp.concatenate(split(toeplitz(taps, rows, 2 * halo + rows, halo - half)), axis=0)
    wide = toeplitz(taps, width, 3 * width, width - half)
    turned = jnp.concatenate(
        [wide[:, (2 - k) * width : (3 - k) * width] for k in range(3)], axis=1
    )
    sideways = jnp.concatenate(split(jnp.where(mirror == 0, wide, turned)), axis=0)

    node_count = levels_w * levels_a
    tables = jnp.concatenate([gain_ref[...], path_ref[...], albedo_ref[...]], axis=0)
    spread_a = lax.broadcasted_iota(jnp.int32, (levels_a, node_count), 0)
    spread_n = lax.broadcasted_iota(jnp.int32, (levels_a, node_count), 1)
    spread = jnp.where(spread_n % levels_a == spread_a, 1.0, 0.0).astype(bf16)
    wide = jnp.dot(tables, spread, preferred_element_type=f32)
    wide_w = lax.broadcasted_iota(jnp.int32, wide.shape, 0) % levels_w
    wide_n = lax.broadcasted_iota(jnp.int32, wide.shape, 1) // levels_a
    wide = jnp.where(wide_w == wide_n, wide, 0.0).astype(bf16)
    table_rows = levels_e * bands
    into = lax.broadcasted_iota(jnp.int32, (3 * table_rows, wide.shape[0]), 0)
    source = lax.broadcasted_iota(jnp.int32, (3 * table_rows, wide.shape[0]), 1) // levels_w
    within = into % table_rows
    wanted = into - within + (within % bands) * levels_e + within // bands
    lut = jnp.dot(
        jnp.where(source == wanted, 1.0, 0.0).astype(bf16), wide, preferred_element_type=f32
    ).astype(bf16)

    for load in loads[8:]:
        load.wait()
    sub = lax.broadcasted_iota(jnp.int32, (8, width), 0)
    lower = sub < bands
    pair_e = (sub // bands).astype(f32)
    per_tile = 8 // bands

    def prepare(index, carry):
        at_cols = pl.ds(pl.multiple_of((index // seg_dev) * width, width), width)
        base = pl.multiple_of((index % seg_dev) * SEG, SEG)
        at_rows = pl.ds(base, SEG)
        vapour = vapour_ref[at_rows, at_cols]
        height = class_ref[at_rows, at_cols].astype(f32) + frac_ref[at_rows, at_cols]
        for w in range(levels_w):
            weights[w, index % seg_dev, :, at_cols] = jnp.maximum(0.0, 1.0 - jnp.abs(vapour - float(w)))
        for row in range(SEG):
            for k in range(table_rows // 8):
                heights[base + row, k, :, at_cols] = jnp.maximum(
                    0.0, 1.0 - jnp.abs(height[row : row + 1] - (pair_e + float(per_tile * k)))
                )
        return carry

    early = seg_dev * chunks * EARLY // 16
    lax.fori_loop(0, early, prepare, 0)
    if pieces > 1:
        start_halo(1)
    lax.fori_loop(early, seg_dev * chunks, prepare, 0)
    if pieces > 2:
        start_halo(2)

    def wait_piece(piece):
        for index, da in enumerate((-1, 1)):

            @pl.when(exists(along - da, n_along))
            def _():
                halo_copy(index, piece).wait_recv()

    def start_side(index):
        @pl.when(exists((inner, outer)[index], n_across))
        def _():
            side_copy(index).start()

    def wait_side(index):
        @pl.when(exists((inner, outer)[index], n_across))
        def _():
            side_copy(index).wait_recv()

    def fall(tile):
        product = jnp.dot(
            down, padded[:, tile * pair : (tile + 1) * pair], preferred_element_type=f32
        )
        high, low = split(product[:rows] + product[rows:])
        at = slice(tile * width, (tile + 1) * width)
        tall[0:rows, at] = high[:, :width]
        tall[rows : 2 * rows, at] = high[:, width:]
        tall[2 * rows : 3 * rows, at] = low[:, :width]
        tall[3 * rows : 4 * rows, at] = low[:, width:]

    def smooth(chunk):
        fresh = [chunk + 2] if chunk else [1, 2, 0]
        for tile in fresh:
            if tile == 0:
                wait_side(1)
            elif tile == chunks + 1:
                wait_side(0)
            elif (tile - 1) % per_piece == 0:
                wait_piece((tile - 1) // per_piece)
                if tile == 1:
                    start_side(1)
                if tile + per_piece == chunks + 1:
                    start_side(0)
            fall(tile)
        product = dot_nt(tall[:, chunk * width : (chunk + 3) * width], sideways)
        smoothed = product[: 2 * rows, :width] + (
            product[2 * rows :, :width] + product[: 2 * rows, width:]
        )
        aerosol = smoothed[:rows] / jnp.maximum(smoothed[rows:], 1.0)
        pos_ref[...] = (levels_a - 1) * jax.nn.sigmoid(aerosol)

    chosen = []
    for number, side in enumerate(SIDES):
        rank = jnp.int32(0)
        first = [jnp.int32(0) for _ in range(CAP)]
        for s in range(seg_dev):
            hit = routes_ref[1, s] - along == side
            for k in range(CAP):
                first[k] = jnp.where(hit & (rank == k), s, first[k])
            rank = rank + jnp.where(hit, 1, 0)
        chosen.append(first)

    node_a = lax.broadcasted_iota(jnp.int32, (levels_a, width), 0).astype(f32)
    quad = 16 // bands
    group = max(1, 256 // width)

    def correct(chunk, seg):
        at_cols = lanes_of(chunk)
        base = pl.multiple_of(seg * SEG, SEG)
        base_flat = pl.multiple_of(seg * seg_rows, seg_rows)
        position = pos_ref[pl.ds(base, SEG), :]
        for first in range(0, SEG, quad):
            partial = []
            values = []
            for start in range(first, first + quad, group):
                joints = []
                for row in range(start, start + group):
                    weight_a = jnp.maximum(0.0, 1.0 - jnp.abs(position[row : row + 1] - node_a))
                    weight_a = weight_a.astype(bf16)
                    joints.append(
                        jnp.concatenate(
                            [
                                weight_a
                                * jnp.broadcast_to(
                                    weights[w, seg, row : row + 1, at_cols], (levels_a, width)
                                ).astype(bf16)
                                for w in range(levels_w)
                            ],
                            axis=0,
                        )
                    )
                joint = joints[0] if group == 1 else jnp.concatenate(joints, axis=1)
                product = jnp.dot(lut, joint, preferred_element_type=f32)
                for k in range(group):
                    values.append(product[:, k * width : (k + 1) * width])
            for row in range(first, first + quad):
                nodes = values[row - first]
                sums = [None] * 3
                for k in range(table_rows // 8):
                    weight_e = heights[base + row, k, :, at_cols]
                    for t in range(3):
                        at = t * table_rows + k * 8
                        term = nodes[at : at + 8] * weight_e
                        sums[t] = term if sums[t] is None else sums[t] + term
                partial.append(sums)
            radiance = toa_ref[pl.ds(base_flat + first * bands, quad * bands), at_cols].astype(f32)
            surfaces = []
            for part in range(quad // 2):
                coefficient = []
                for t in range(3):
                    one, two = partial[2 * part][t], partial[2 * part + 1][t]
                    kept = jnp.where(lower, one, two)
                    moved = pltpu.roll(jnp.where(lower, two, one), bands, 0)
                    coefficient.append(kept + moved)
                scaled = coefficient[0] * radiance[part * 8 : part * 8 + 8] - coefficient[1]
                surfaces.append(scaled / (1.0 + coefficient[2] * scaled))
            corrected[chunk, seg, first * bands : (first + quad) * bands, :] = jnp.concatenate(
                surfaces, axis=0
            ).astype(bf16)

    def correct_all(chunk):
        def step(seg, carry):
            correct(chunk, seg)
            return carry

        lax.fori_loop(0, seg_dev, step, 0, unroll=True)

    def fill_slots(chunk):
        for number in range(len(SIDES)):
            for k in range(CAP):
                into = (number * CAP + k) * seg_rows
                slots[chunk, into : into + seg_rows] = corrected[chunk, chosen[number][k]]

    def start_slot(chunk, number, wanted):
        @pl.when(exists(along + SIDES[number], n_along) & wanted)
        def _():
            slot_copy(chunk, number).start()

    odd = along % 2 == 1
    even = jnp.logical_not(odd)
    near = {number: odd if side < 0 else even for number, side in enumerate(SIDES)}

    def start_slots(chunk):
        for number, side in enumerate(SIDES):
            if abs(side) == 1:
                start_slot(chunk, number, near[number])
        for number, side in enumerate(SIDES):
            if abs(side) != 1:
                start_slot(chunk, number, True)
        start_far(chunk, mirror != 0)
        if chunk >= DEFER:
            start_far(chunk - DEFER, mirror == 0)

    def start_far(chunk, wanted):
        for number, side in enumerate(SIDES):
            if abs(side) == 1:
                start_slot(chunk, number, jnp.logical_not(near[number]) & wanted)

    def placed(target):
        row = lax.broadcasted_iota(jnp.int32, (own_rows, target.shape[1]), 0).astype(f32)
        return jnp.where(row == target, 1.0, 0.0).astype(bf16)

    def make_place():
        lane = lax.broadcasted_iota(jnp.int32, (1, own_rows), 1)
        target = jnp.full((1, own_rows), -1, jnp.int32)
        for s in range(seg_dev):
            inside = (lane >= s * seg_rows) & (lane < (s + 1) * seg_rows)
            inside = inside & (routes_ref[0, s] == along)
            target = jnp.where(inside, starts_ref[0, s] * bands + lane - s * seg_rows, target)
        place[:, 0:own_rows] = placed(target.astype(f32))
        tags_wait(come_first, come_count, False)
        for number in order:
            begin = own_rows + number * CAP * seg_rows
            place[:, begin : begin + CAP * seg_rows] = placed(got_tags[number, 0:1, :])
        ones = jnp.ones((place.shape[1], width), bf16)
        count = jnp.dot(place[...], ones, preferred_element_type=f32)
        scale[...] = jnp.maximum(count, 1.0)

    def arrived(first, count):
        for chunk in range(first, first + count):
            slots_wait(come_first, come_count, chunk)

    def put(first, count):
        arrived(first, count)
        segments = [
            jnp.concatenate([corrected[chunk].reshape(own_rows, width), got_rows[chunk]], axis=0)
            for chunk in range(first, first + count)
        ]
        segments = segments[0] if count == 1 else jnp.concatenate(segments, axis=1)
        for k, result in enumerate(averages(place[...], segments, scale[...], bands)):
            out_ref[:, :, lanes_of(first + k)] = result

    for chunk in range(chunks):
        smooth(chunk)
        if chunk == 0:
            for piece in range(3, pieces):
                start_halo(piece)
        if chunk > 1:
            start_slots(chunk - 1)
        correct_all(chunk)
        fill_slots(chunk)
        if chunk == 0:
            make_place()
            if chunks > 1:
                start_slots(0)
    start_slots(chunks - 1)
    for chunk in range(chunks - min(DEFER, chunks), chunks):
        start_far(chunk, mirror == 0)
    rest = rest_ref.shape[1] // width
    for k in range(rest):
        mine = corrected[chunks - rest + k].reshape(own_rows, width)
        rest_ref[0:own_rows, k * width : (k + 1) * width] = mine
    for first in range(0, chunks - rest, 2):
        put(first, min(2, chunks - rest - first))
    arrived(chunks - rest, rest)
    for k in range(rest):
        rest_ref[own_rows:, k * width : (k + 1) * width] = got_rows[chunks - rest + k]

    for index, da in enumerate((-1, 1)):

        @pl.when(exists(along + da, n_along))
        def _():
            halo_whole(index).wait_send()

    for index, peer in enumerate((inner, outer)):

        @pl.when(exists(peer, n_across))
        def _():
            side_copy(index).wait_send()

    tags_wait(gone_first, gone_count, True)
    slots_wait(gone_first, gone_count, None)


def store_kernel(bands, done_ref, rest_ref, place, scale, out_hbm, last, sem):
    rows, _, cols = out_hbm.shape
    width = scale.shape[1]
    rest = rest_ref.shape[1]
    mirror = lax.axis_index("across") % 2
    at = pl.ds(pl.multiple_of(jnp.where(mirror == 0, 0, rest), width), cols - rest)
    parts = sem.shape[0] - 1
    copies = []
    for part in range(parts):
        own = slice(part * rows // parts, (part + 1) * rows // parts)
        copies.append(
            pltpu.make_async_copy(done_ref.at[own, :, at], out_hbm.at[own, :, at], sem.at[part])
        )
    if rest < cols:
        for copy in copies:
            copy.start()
    pieces = averages(place[...], rest_ref[...], scale[...], bands)
    for k, result in enumerate(pieces):
        spot = jnp.where(mirror == 0, k, rest // width - 1 - k) * width
        last[:, :, pl.ds(pl.multiple_of(spot, width), width)] = result
    at = pl.ds(pl.multiple_of(jnp.where(mirror == 0, cols - rest, 0), width), rest)
    final = pltpu.make_async_copy(last, out_hbm.at[:, :, at], sem.at[parts])
    final.start()
    if rest < cols:
        for copy in copies:
            copy.wait()
    final.wait()


def body(
    n_along,
    n_across,
    toa_bands,
    dark_mask,
    vapour,
    elev_class,
    elev_frac,
    kernel,
    lut_gain,
    lut_path,
    lut_albedo,
    routes,
    starts,
):
    rows, bands, cols = toa_bands.shape
    half = kernel.shape[0] // 2
    halo = -(-half // 16) * 16
    levels = lut_gain.shape[1:]
    levels_e, levels_a, levels_w = levels
    seg_dev = routes.shape[0]
    seg_rows = SEG * bands
    side_count = len(SIDES)
    width = math.gcd(cols, WIDTH)
    chunks = cols // width
    pieces = chunks // math.gcd(chunks, 2)
    vmem = pl.BlockSpec(memory_space=pltpu.VMEM)
    hbm = pl.BlockSpec(memory_space=pltpu.HBM)
    table_shape = (bands * levels_e * levels_w, levels_a)
    dma = pltpu.SemaphoreType.DMA

    def table(lut):
        return lut.transpose(0, 1, 3, 2).reshape(table_shape)

    rest = width * (2 - chunks % 2)
    held = (rows * bands, rows * bands + side_count * CAP * seg_rows)
    made = (
        jax.ShapeDtypeStruct((rows, bands, cols), bf16),
        jax.ShapeDtypeStruct((held[1], rest), bf16),
        jax.ShapeDtypeStruct(held, bf16),
        jax.ShapeDtypeStruct((rows * bands, width), f32),
    )
    parts = pl.pallas_call(
        functools.partial(main_kernel, n_along, n_across, bands, levels),
        out_shape=made,
        in_specs=[hbm] * 11,
        out_specs=[vmem] * 4,
        scratch_shapes=[
            pltpu.SMEM((2, seg_dev), jnp.int32),
            pltpu.SMEM((2, seg_dev), jnp.int32),
            pltpu.VMEM((rows, bands, cols), bf16),
            pltpu.VMEM((rows, cols), jnp.int32),
            pltpu.VMEM((1, kernel.shape[0]), f32),
            pltpu.VMEM(table_shape, bf16),
            pltpu.VMEM(table_shape, bf16),
            pltpu.VMEM(table_shape, bf16),
            pltpu.VMEM((rows, cols), f32),
            pltpu.VMEM((rows, cols), jnp.int32),
            pltpu.VMEM((rows, cols), f32),
            pltpu.VMEM((rows * bands, cols), bf16),
            pltpu.VMEM((side_count, 8, CAP * seg_rows), f32),
            pltpu.VMEM((8, LANES), f32),
            pltpu.VMEM((rows + 2 * halo, (chunks + 2) * 2 * width), bf16),
            pltpu.VMEM((4 * rows, (chunks + 2) * width), bf16),
            pltpu.VMEM((rows, width), f32),
            pltpu.VMEM((levels_w, seg_dev, SEG, cols), f32),
            pltpu.VMEM((rows, levels_e * bands // 8, 8, cols), f32),
            pltpu.VMEM((chunks, seg_dev, seg_rows, width), bf16),
            pltpu.VMEM((chunks, side_count * CAP * seg_rows, width), bf16),
            pltpu.VMEM((chunks, side_count * CAP * seg_rows, width), bf16),
            pltpu.VMEM((side_count, 8, CAP * seg_rows), f32),
            dma((7,)),
            dma((2,)),
            dma((2, pieces)),
            dma((2,)),
            dma((2,)),
            dma,
            dma,
            dma,
            dma((chunks,)),
        ],
        compiler_params=pltpu.CompilerParams(
            collective_id=0, has_side_effects=True, vmem_limit_bytes=44 * 1024 * 1024
        ),
        name="main",
    )(
        *(
            pltpu.with_memory_space_constraint(value, pltpu.HBM)
            for value in (
                routes.T,
                starts.T,
                toa_bands,
                dark_mask,
                kernel[None],
                table(lut_gain),
                table(lut_path),
                table(lut_albedo),
                vapour,
                elev_class,
                elev_frac,
            )
        ),
    )
    out = pl.pallas_call(
        functools.partial(store_kernel, bands),
        out_shape=made[0],
        in_specs=[vmem] * 4,
        out_specs=hbm,
        scratch_shapes=[
            pltpu.VMEM((rows, bands, rest), bf16),
            dma((1 + math.gcd(rows, 4),)),
        ],
        name="store",
    )(*(pltpu.with_memory_space_constraint(value, pltpu.VMEM) for value in parts))
    return out[None]


def solution(mesh):
    in_specs = (
        P(("groups", "along"), None, "across"),
        P(("groups", "along"), "across"),
        P(("groups", "along"), "across"),
        P(("groups", "along"), "across"),
        P(("groups", "along"), "across"),
        P(),
        P(),
        P(),
        P(),
        P(("groups", "along"), None),
        P(("groups", "along"), None),
    )
    out_specs = P(("groups", "along"), None, None, "across")
    run = functools.partial(body, mesh.shape["along"], mesh.shape["across"])
    return jax.shard_map(run, mesh=mesh, in_specs=in_specs, out_specs=out_specs, check_vma=False)
```

```python
import functools
import math

import jax
import jax.numpy as jnp
from jax import lax
from jax.experimental import pallas as pl
from jax.experimental.pallas import tpu as pltpu
from jax.sharding import PartitionSpec as P

SEG = 16
REACH = 2
CAP = 2
LANES = 128
WIDTH = 128
MESH_ID = pl.DeviceIdType.MESH
SIDES = [side - REACH for side in range(REACH)] + [side + 1 for side in range(REACH)]
EARLY = 5
DEFER = 4
f32 = jnp.float32
bf16 = jnp.bfloat16


def split(value):
    high = value.astype(bf16)
    return high, (value - high.astype(f32)).astype(bf16)


def toeplitz(taps, row_count, width, first):
    line = jnp.broadcast_to(taps, (8, taps.shape[1]))
    if width > taps.shape[1]:
        line = jnp.concatenate([line, jnp.zeros((8, width - taps.shape[1]), f32)], axis=1)
    stair = pltpu.roll(line, 0, 1, stride=1, stride_axis=0)
    return jnp.concatenate(
        [pltpu.roll(stair, first + 8 * group, 1) for group in range(row_count // 8)], axis=0
    )


def dot_nt(left, right):
    return lax.dot_general(left, right, (((1,), (1,)), ((), ())), preferred_element_type=f32)


def averages(place, segments, scale, bands):
    width = scale.shape[1]
    summed = jnp.dot(place, segments, preferred_element_type=f32)
    for k in range(segments.shape[1] // width):
        result = summed[:, k * width : (k + 1) * width] / scale
        yield result.reshape(-1, bands, width).astype(bf16)


def exists(position, count):
    return (position >= 0) & (position < count)


def main_kernel(
    n_along,
    n_across,
    bands,
    levels,
    routes_hbm,
    starts_hbm,
    toa_hbm,
    mask_hbm,
    taps_hbm,
    gain_hbm,
    path_hbm,
    albedo_hbm,
    vapour_hbm,
    class_hbm,
    frac_hbm,
    out_ref,
    rest_ref,
    place,
    scale,
    routes_ref,
    starts_ref,
    raw_ref,
    mask_ref,
    taps_ref,
    gain_ref,
    path_ref,
    albedo_ref,
    vapour_ref,
    class_ref,
    frac_ref,
    toa_ref,
    tags_ref,
    taps_pad,
    padded,
    tall,
    pos_ref,
    weights,
    heights,
    corrected,
    slots,
    got_rows,
    got_tags,
    load_sem,
    halo_send,
    halo_recv,
    side_send,
    side_recv,
    tag_send,
    tag_recv,
    slot_send,
    slot_recv,
):
    along, across = lax.axis_index("along"), lax.axis_index("across")
    levels_e, levels_a, levels_w = levels
    rows, _, cols = toa_hbm.shape
    halo = (padded.shape[0] - rows) // 2
    half = taps_hbm.shape[1] // 2
    width = slots.shape[2]
    chunks = cols // width
    seg_rows = SEG * bands
    seg_dev = rows // SEG
    own_rows = rows * bands
    pair = 2 * width
    mirror = across % 2
    inner = across + 1 - 2 * mirror
    outer = across - 1 + 2 * mirror
    pieces = halo_recv.shape[1]
    per_piece = chunks // pieces

    def lanes_of(chunk):
        at = jnp.where(mirror == 0, chunk, chunks - 1 - chunk) * width
        return pl.ds(pl.multiple_of(at, width), width)

    loads = [
        pltpu.make_async_copy(source, target, load_sem.at[number if number < 4 else number - 4])
        for number, (source, target) in enumerate(
            (
                (routes_hbm, routes_ref),
                (starts_hbm, starts_ref),
                (toa_hbm, raw_ref),
                (mask_hbm, mask_ref),
                (taps_hbm, taps_ref),
                (gain_hbm, gain_ref),
                (path_hbm, path_ref),
                (albedo_hbm, albedo_ref),
                (vapour_hbm, vapour_ref),
                (class_hbm, class_ref),
                (frac_hbm, frac_ref),
            )
        )
    ]
    for load in loads[:4]:
        load.start()
    barrier = pltpu.get_barrier_semaphore()
    peers = [
        (exists(along + da, n_along), {"along": along + da})
        for da in sorted({-1, 1, *SIDES}, key=abs)
    ]
    peers += [
        (exists(inner, n_across), {"across": inner}),
        (exists(outer, n_across), {"across": outer}),
    ]
    for present, peer in peers:

        @pl.when(present)
        def _():
            pl.semaphore_signal(barrier, inc=1, device_id=peer, device_id_type=MESH_ID)

    row = lax.broadcasted_iota(jnp.int32, (rows, rows * bands), 0) * bands
    col = lax.broadcasted_iota(jnp.int32, (rows, rows * bands), 1)
    pick = jnp.where(col == row, 8.0, 0.0) + jnp.where(col == row + 2, -4.0, 0.0)
    for load in loads[:4]:
        load.wait()
    for load in loads[4:]:
        load.start()
    flat = raw_ref[...].astype(f32).reshape(rows * bands, cols).astype(bf16)
    toa_ref[...] = flat
    value = jnp.dot(pick.astype(bf16), flat, preferred_element_type=f32)
    darkness = mask_ref[...].astype(f32)
    weighted = (darkness * value).astype(bf16)
    darkness = darkness.astype(bf16)
    for tile in range(chunks):
        own = slice(tile * width, (tile + 1) * width)
        at = pl.multiple_of((jnp.where(mirror == 0, tile, chunks - 1 - tile) + 1) * pair, pair)
        padded[halo : halo + rows, pl.ds(at, width)] = weighted[:, own]
        padded[halo : halo + rows, pl.ds(at + width, width)] = darkness[:, own]

    lane = lax.broadcasted_iota(jnp.int32, (8, CAP * seg_rows), 1)
    for number, side in enumerate(SIDES):
        target = jnp.full((8, CAP * seg_rows), -1, jnp.int32)
        rank = jnp.int32(0)
        for s in range(seg_dev):
            hit = routes_ref[1, s] - along == side
            spot = jnp.where(hit, rank, -1)
            inside = (lane >= spot * seg_rows) & (lane < (spot + 1) * seg_rows) & (spot >= 0)
            target = jnp.where(inside, starts_ref[1, s] * bands + lane - spot * seg_rows, target)
            rank = rank + jnp.where(hit, 1, 0)
        tags_ref[number] = target.astype(f32)

    spans = {
        -1: (slice(halo, 2 * halo), slice(halo + rows, 2 * halo + rows)),
        1: (slice(rows, halo + rows), slice(0, halo)),
    }

    def halo_copy(index, piece):
        da = (-1, 1)[index]
        begin = (1 + piece * per_piece) * pair
        at = slice(begin, begin + per_piece * pair)
        return pltpu.make_async_remote_copy(
            src_ref=padded.at[spans[da][0], at],
            dst_ref=padded.at[spans[da][1], at],
            send_sem=halo_send.at[index],
            recv_sem=halo_recv.at[index, piece],
            device_id={"along": along + da},
            device_id_type=MESH_ID,
        )

    def halo_whole(index):
        da = (-1, 1)[index]
        at = slice(pair, (1 + chunks) * pair)
        return pltpu.make_async_remote_copy(
            src_ref=padded.at[spans[da][0], at],
            dst_ref=padded.at[spans[da][1], at],
            send_sem=halo_send.at[index],
            recv_sem=halo_recv.at[index, 0],
            device_id={"along": along + da},
            device_id_type=MESH_ID,
        )

    def side_copy(index):
        source, target = ((chunks, chunks + 1), (1, 0))[index]
        return pltpu.make_async_remote_copy(
            src_ref=padded.at[:, source * pair : (source + 1) * pair],
            dst_ref=padded.at[:, target * pair : (target + 1) * pair],
            send_sem=side_send.at[index],
            recv_sem=side_recv.at[index],
            device_id={"across": (inner, outer)[index]},
            device_id_type=MESH_ID,
        )

    def tag_copy(number):
        return pltpu.make_async_remote_copy(
            src_ref=tags_ref.at[number],
            dst_ref=got_tags.at[number],
            send_sem=tag_send,
            recv_sem=tag_recv,
            device_id={"along": along + SIDES[number]},
            device_id_type=MESH_ID,
        )

    def slot_copy(chunk, number):
        count = CAP * seg_rows
        return pltpu.make_async_remote_copy(
            src_ref=slots.at[chunk, number * count : (number + 1) * count],
            dst_ref=got_rows.at[chunk, number * count : (number + 1) * count],
            send_sem=slot_send,
            recv_sem=slot_recv.at[chunk],
            device_id={"along": along + SIDES[number]},
            device_id_type=MESH_ID,
        )

    def count_of(flags):
        return sum(flag.astype(jnp.int32) for flag in flags)

    half_count = len(SIDES) // 2
    gone = [exists(along + side, n_along) for side in SIDES]
    come = [exists(along - side, n_along) for side in SIDES]
    gone_first = half_count - count_of(gone[:half_count])
    come_first = half_count - count_of(come[:half_count])
    gone_count, come_count = count_of(gone), count_of(come)
    per_side = CAP * seg_rows

    def tags_wait(first, count, sent):
        for k in range(1, len(SIDES) + 1):

            @pl.when(count == k)
            def _():
                copy = pltpu.make_async_remote_copy(
                    src_ref=tags_ref.at[pl.ds(first, k)],
                    dst_ref=got_tags.at[pl.ds(first, k)],
                    send_sem=tag_send,
                    recv_sem=tag_recv,
                    device_id={"along": along},
                    device_id_type=MESH_ID,
                )
                if sent:
                    copy.wait_send()
                else:
                    copy.wait_recv()

    def slots_wait(first, count, chunk):
        for k in range(1, len(SIDES) + 1):

            @pl.when(count == k)
            def _():
                at = pl.ds(pl.multiple_of(first * per_side, per_side), k * per_side)
                which = slice(0, chunks) if chunk is None else chunk
                copy = pltpu.make_async_remote_copy(
                    src_ref=slots.at[which, at],
                    dst_ref=got_rows.at[which, at],
                    send_sem=slot_send,
                    recv_sem=slot_recv.at[0 if chunk is None else chunk],
                    device_id={"along": along},
                    device_id_type=MESH_ID,
                )
                if chunk is None:
                    copy.wait_send()
                else:
                    copy.wait_recv()

    def start_halo(piece):
        for index, da in enumerate((-1, 1)):

            @pl.when(exists(along + da, n_along))
            def _():
                halo_copy(index, piece).start()

    pl.semaphore_wait(barrier, sum(present.astype(jnp.int32) for present, _ in peers))
    start_halo(0)
    order = sorted(range(len(SIDES)), key=lambda number: abs(SIDES[number]))
    for number in order:

        @pl.when(exists(along + SIDES[number], n_along))
        def _():
            tag_copy(number).start()

        @pl.when(jnp.logical_not(exists(along - SIDES[number], n_along)))
        def _():
            begin = number * CAP * seg_rows
            got_rows[:, begin : begin + CAP * seg_rows, :] = jnp.zeros(
                (chunks, CAP * seg_rows, width), bf16
            )
            got_tags[number] = jnp.full(got_tags.shape[1:], -1.0, f32)

    for da in (-1, 1):

        @pl.when(jnp.logical_not(exists(along - da, n_along)))
        def _():
            padded[spans[da][1], pair : (chunks + 1) * pair] = jnp.zeros(
                (halo, chunks * pair), bf16
            )

    for index, (peer, target) in enumerate(((inner, chunks + 1), (outer, 0))):

        @pl.when(jnp.logical_not(exists(peer, n_across)))
        def _():
            padded[:, target * pair : (target + 1) * pair] = jnp.zeros(
                (padded.shape[0], pair), bf16
            )

    for load in loads[4:8]:
        load.wait()
    taps_pad[...] = jnp.zeros(taps_pad.shape, f32)
    taps_pad[0:1, 0 : taps_ref.shape[1]] = taps_ref[...]
    taps = taps_pad[0:1, :]
    down = jnp.concatenate(split(toeplitz(taps, rows, 2 * halo + rows, halo - half)), axis=0)
    wide = toeplitz(taps, width, 3 * width, width - half)
    turned = jnp.concatenate(
        [wide[:, (2 - k) * width : (3 - k) * width] for k in range(3)], axis=1
    )
    sideways = jnp.concatenate(split(jnp.where(mirror == 0, wide, turned)), axis=0)

    node_count = levels_w * levels_a
    tables = jnp.concatenate([gain_ref[...], path_ref[...], albedo_ref[...]], axis=0)
    spread_a = lax.broadcasted_iota(jnp.int32, (levels_a, node_count), 0)
    spread_n = lax.broadcasted_iota(jnp.int32, (levels_a, node_count), 1)
    spread = jnp.where(spread_n % levels_a == spread_a, 1.0, 0.0).astype(bf16)
    wide = jnp.dot(tables, spread, preferred_element_type=f32)
    wide_w = lax.broadcasted_iota(jnp.int32, wide.shape, 0) % levels_w
    wide_n = lax.broadcasted_iota(jnp.int32, wide.shape, 1) // levels_a
    wide = jnp.where(wide_w == wide_n, wide, 0.0).astype(bf16)
    table_rows = levels_e * bands
    into = lax.broadcasted_iota(jnp.int32, (3 * table_rows, wide.shape[0]), 0)
    source = lax.broadcasted_iota(jnp.int32, (3 * table_rows, wide.shape[0]), 1) // levels_w
    within = into % table_rows
    wanted = into - within + (within % bands) * levels_e + within // bands
    lut = jnp.dot(
        jnp.where(source == wanted, 1.0, 0.0).astype(bf16), wide, preferred_element_type=f32
    ).astype(bf16)

    for load in loads[8:]:
        load.wait()
    sub = lax.broadcasted_iota(jnp.int32, (8, width), 0)
    lower = sub < bands
    pair_e = (sub // bands).astype(f32)
    per_tile = 8 // bands

    def prepare(index, carry):
        at_cols = pl.ds(pl.multiple_of((index // seg_dev) * width, width), width)
        base = pl.multiple_of((index % seg_dev) * SEG, SEG)
        at_rows = pl.ds(base, SEG)
        vapour = vapour_ref[at_rows, at_cols]
        height = class_ref[at_rows, at_cols].astype(f32) + frac_ref[at_rows, at_cols]
        for w in range(levels_w):
            weights[w, index % seg_dev, :, at_cols] = jnp.maximum(0.0, 1.0 - jnp.abs(vapour - float(w)))
        for row in range(SEG):
            for k in range(table_rows // 8):
                heights[base + row, k, :, at_cols] = jnp.maximum(
                    0.0, 1.0 - jnp.abs(height[row : row + 1] - (pair_e + float(per_tile * k)))
                )
        return carry

    early = seg_dev * chunks * EARLY // 16
    lax.fori_loop(0, early, prepare, 0)
    if pieces > 1:
        start_halo(1)
    lax.fori_loop(early, seg_dev * chunks, prepare, 0)
    if pieces > 2:
        start_halo(2)

    def wait_piece(piece):
        for index, da in enumerate((-1, 1)):

            @pl.when(exists(along - da, n_along))
            def _():
                halo_copy(index, piece).wait_recv()

    def start_side(index):
        @pl.when(exists((inner, outer)[index], n_across))
        def _():
            side_copy(index).start()

    def wait_side(index):
        @pl.when(exists((inner, outer)[index], n_across))
        def _():
            side_copy(index).wait_recv()

    def fall(tile):
        product = jnp.dot(
            down, padded[:, tile * pair : (tile + 1) * pair], preferred_element_type=f32
        )
        high, low = split(product[:rows] + product[rows:])
        at = slice(tile * width, (tile + 1) * width)
        tall[0:rows, at] = high[:, :width]
        tall[rows : 2 * rows, at] = high[:, width:]
        tall[2 * rows : 3 * rows, at] = low[:, :width]
        tall[3 * rows : 4 * rows, at] = low[:, width:]

    def smooth(chunk):
        fresh = [chunk + 2] if chunk else [1, 2, 0]
        for tile in fresh:
            if tile == 0:
                wait_side(1)
            elif tile == chunks + 1:
                wait_side(0)
            elif (tile - 1) % per_piece == 0:
                wait_piece((tile - 1) // per_piece)
                if tile == 1:
                    start_side(1)
                if tile + per_piece == chunks + 1:
                    start_side(0)
            fall(tile)
        product = dot_nt(tall[:, chunk * width : (chunk + 3) * width], sideways)
        smoothed = product[: 2 * rows, :width] + (
            product[2 * rows :, :width] + product[: 2 * rows, width:]
        )
        aerosol = smoothed[:rows] / jnp.maximum(smoothed[rows:], 1.0)
        pos_ref[...] = (levels_a - 1) * jax.nn.sigmoid(aerosol)

    chosen = []
    for number, side in enumerate(SIDES):
        rank = jnp.int32(0)
        first = [jnp.int32(0) for _ in range(CAP)]
        for s in range(seg_dev):
            hit = routes_ref[1, s] - along == side
            for k in range(CAP):
                first[k] = jnp.where(hit & (rank == k), s, first[k])
            rank = rank + jnp.where(hit, 1, 0)
        chosen.append(first)

    node_a = lax.broadcasted_iota(jnp.int32, (levels_a, width), 0).astype(f32)
    quad = 16 // bands
    group = max(1, 256 // width)

    def correct(chunk, seg):
        at_cols = lanes_of(chunk)
        base = pl.multiple_of(seg * SEG, SEG)
        base_flat = pl.multiple_of(seg * seg_rows, seg_rows)
        position = pos_ref[pl.ds(base, SEG), :]
        for first in range(0, SEG, quad):
            partial = []
            values = []
            for start in range(first, first + quad, group):
                joints = []
                for row in range(start, start + group):
                    weight_a = jnp.maximum(0.0, 1.0 - jnp.abs(position[row : row + 1] - node_a))
                    weight_a = weight_a.astype(bf16)
                    joints.append(
                        jnp.concatenate(
                            [
                                weight_a
                                * jnp.broadcast_to(
                                    weights[w, seg, row : row + 1, at_cols], (levels_a, width)
                                ).astype(bf16)
                                for w in range(levels_w)
                            ],
                            axis=0,
                        )
                    )
                joint = joints[0] if group == 1 else jnp.concatenate(joints, axis=1)
                product = jnp.dot(lut, joint, preferred_element_type=f32)
                for k in range(group):
                    values.append(product[:, k * width : (k + 1) * width])
            for row in range(first, first + quad):
                nodes = values[row - first]
                sums = [None] * 3
                for k in range(table_rows // 8):
                    weight_e = heights[base + row, k, :, at_cols]
                    for t in range(3):
                        at = t * table_rows + k * 8
                        term = nodes[at : at + 8] * weight_e
                        sums[t] = term if sums[t] is None else sums[t] + term
                partial.append(sums)
            radiance = toa_ref[pl.ds(base_flat + first * bands, quad * bands), at_cols].astype(f32)
            surfaces = []
            for part in range(quad // 2):
                coefficient = []
                for t in range(3):
                    one, two = partial[2 * part][t], partial[2 * part + 1][t]
                    kept = jnp.where(lower, one, two)
                    moved = pltpu.roll(jnp.where(lower, two, one), bands, 0)
                    coefficient.append(kept + moved)
                scaled = coefficient[0] * radiance[part * 8 : part * 8 + 8] - coefficient[1]
                surfaces.append(scaled / (1.0 + coefficient[2] * scaled))
            corrected[chunk, seg, first * bands : (first + quad) * bands, :] = jnp.concatenate(
                surfaces, axis=0
            ).astype(bf16)

    def correct_all(chunk):
        def step(seg, carry):
            correct(chunk, seg)
            return carry

        lax.fori_loop(0, seg_dev, step, 0, unroll=True)

    def fill_slots(chunk):
        for number in range(len(SIDES)):
            for k in range(CAP):
                into = (number * CAP + k) * seg_rows
                slots[chunk, into : into + seg_rows] = corrected[chunk, chosen[number][k]]

    def start_slot(chunk, number, wanted):
        @pl.when(exists(along + SIDES[number], n_along) & wanted)
        def _():
            slot_copy(chunk, number).start()

    odd = along % 2 == 1
    even = jnp.logical_not(odd)
    near = {number: odd if side < 0 else even for number, side in enumerate(SIDES)}

    def start_slots(chunk):
        for number, side in enumerate(SIDES):
            if abs(side) == 1:
                start_slot(chunk, number, near[number])
        for number, side in enumerate(SIDES):
            if abs(side) != 1:
                start_slot(chunk, number, True)
        start_far(chunk, mirror != 0)
        if chunk >= DEFER:
            start_far(chunk - DEFER, mirror == 0)

    def start_far(chunk, wanted):
        for number, side in enumerate(SIDES):
            if abs(side) == 1:
                start_slot(chunk, number, jnp.logical_not(near[number]) & wanted)

    def placed(target):
        row = lax.broadcasted_iota(jnp.int32, (own_rows, target.shape[1]), 0).astype(f32)
        return jnp.where(row == target, 1.0, 0.0).astype(bf16)

    def make_place():
        lane = lax.broadcasted_iota(jnp.int32, (1, own_rows), 1)
        target = jnp.full((1, own_rows), -1, jnp.int32)
        for s in range(seg_dev):
            inside = (lane >= s * seg_rows) & (lane < (s + 1) * seg_rows)
            inside = inside & (routes_ref[0, s] == along)
            target = jnp.where(inside, starts_ref[0, s] * bands + lane - s * seg_rows, target)
        place[:, 0:own_rows] = placed(target.astype(f32))
        tags_wait(come_first, come_count, False)
        for number in order:
            begin = own_rows + number * CAP * seg_rows
            place[:, begin : begin + CAP * seg_rows] = placed(got_tags[number, 0:1, :])
        ones = jnp.ones((place.shape[1], width), bf16)
        count = jnp.dot(place[...], ones, preferred_element_type=f32)
        scale[...] = jnp.maximum(count, 1.0)

    def arrived(first, count):
        for chunk in range(first, first + count):
            slots_wait(come_first, come_count, chunk)

    def put(first, count):
        arrived(first, count)
        segments = [
            jnp.concatenate([corrected[chunk].reshape(own_rows, width), got_rows[chunk]], axis=0)
            for chunk in range(first, first + count)
        ]
        segments = segments[0] if count == 1 else jnp.concatenate(segments, axis=1)
        for k, result in enumerate(averages(place[...], segments, scale[...], bands)):
            out_ref[:, :, lanes_of(first + k)] = result

    for chunk in range(chunks):
        smooth(chunk)
        if chunk > 1:
            start_slots(chunk - 1)
        correct_all(chunk)
        if chunk == 0:
            for piece in range(3, pieces):
                start_halo(piece)
        fill_slots(chunk)
        if chunk == 0:
            make_place()
            if chunks > 1:
                start_slots(0)
    start_slots(chunks - 1)
    for chunk in range(chunks - min(DEFER, chunks), chunks):
        start_far(chunk, mirror == 0)
    rest = rest_ref.shape[1] // width
    for k in range(rest):
        mine = corrected[chunks - rest + k].reshape(own_rows, width)
        rest_ref[0:own_rows, k * width : (k + 1) * width] = mine
    for first in range(0, chunks - rest, 2):
        put(first, min(2, chunks - rest - first))
    arrived(chunks - rest, rest)
    for k in range(rest):
        rest_ref[own_rows:, k * width : (k + 1) * width] = got_rows[chunks - rest + k]

    for index, da in enumerate((-1, 1)):

        @pl.when(exists(along + da, n_along))
        def _():
            halo_whole(index).wait_send()

    for index, peer in enumerate((inner, outer)):

        @pl.when(exists(peer, n_across))
        def _():
            side_copy(index).wait_send()

    tags_wait(gone_first, gone_count, True)
    slots_wait(gone_first, gone_count, None)


def store_kernel(bands, done_ref, rest_ref, place, scale, out_hbm, last, sem):
    rows, _, cols = out_hbm.shape
    width = scale.shape[1]
    rest = rest_ref.shape[1]
    mirror = lax.axis_index("across") % 2
    at = pl.ds(pl.multiple_of(jnp.where(mirror == 0, 0, rest), width), cols - rest)
    parts = sem.shape[0] - 1
    copies = []
    for part in range(parts):
        own = slice(part * rows // parts, (part + 1) * rows // parts)
        copies.append(
            pltpu.make_async_copy(done_ref.at[own, :, at], out_hbm.at[own, :, at], sem.at[part])
        )
    if rest < cols:
        for copy in copies:
            copy.start()
    pieces = averages(place[...], rest_ref[...], scale[...], bands)
    for k, result in enumerate(pieces):
        spot = jnp.where(mirror == 0, k, rest // width - 1 - k) * width
        last[:, :, pl.ds(pl.multiple_of(spot, width), width)] = result
    at = pl.ds(pl.multiple_of(jnp.where(mirror == 0, cols - rest, 0), width), rest)
    final = pltpu.make_async_copy(last, out_hbm.at[:, :, at], sem.at[parts])
    final.start()
    if rest < cols:
        for copy in copies:
            copy.wait()
    final.wait()


def body(
    n_along,
    n_across,
    toa_bands,
    dark_mask,
    vapour,
    elev_class,
    elev_frac,
    kernel,
    lut_gain,
    lut_path,
    lut_albedo,
    routes,
    starts,
):
    rows, bands, cols = toa_bands.shape
    half = kernel.shape[0] // 2
    halo = -(-half // 16) * 16
    levels = lut_gain.shape[1:]
    levels_e, levels_a, levels_w = levels
    seg_dev = routes.shape[0]
    seg_rows = SEG * bands
    side_count = len(SIDES)
    width = math.gcd(cols, WIDTH)
    chunks = cols // width
    pieces = chunks // math.gcd(chunks, 2)
    vmem = pl.BlockSpec(memory_space=pltpu.VMEM)
    hbm = pl.BlockSpec(memory_space=pltpu.HBM)
    table_shape = (bands * levels_e * levels_w, levels_a)
    dma = pltpu.SemaphoreType.DMA

    def table(lut):
        return lut.transpose(0, 1, 3, 2).reshape(table_shape)

    rest = width
    held = (rows * bands, rows * bands + side_count * CAP * seg_rows)
    made = (
        jax.ShapeDtypeStruct((rows, bands, cols), bf16),
        jax.ShapeDtypeStruct((held[1], rest), bf16),
        jax.ShapeDtypeStruct(held, bf16),
        jax.ShapeDtypeStruct((rows * bands, width), f32),
    )
    parts = pl.pallas_call(
        functools.partial(main_kernel, n_along, n_across, bands, levels),
        out_shape=made,
        in_specs=[hbm] * 11,
        out_specs=[vmem] * 4,
        scratch_shapes=[
            pltpu.SMEM((2, seg_dev), jnp.int32),
            pltpu.SMEM((2, seg_dev), jnp.int32),
            pltpu.VMEM((rows, bands, cols), bf16),
            pltpu.VMEM((rows, cols), jnp.int32),
            pltpu.VMEM((1, kernel.shape[0]), f32),
            pltpu.VMEM(table_shape, bf16),
            pltpu.VMEM(table_shape, bf16),
            pltpu.VMEM(table_shape, bf16),
            pltpu.VMEM((rows, cols), f32),
            pltpu.VMEM((rows, cols), jnp.int32),
            pltpu.VMEM((rows, cols), f32),
            pltpu.VMEM((rows * bands, cols), bf16),
            pltpu.VMEM((side_count, 8, CAP * seg_rows), f32),
            pltpu.VMEM((8, LANES), f32),
            pltpu.VMEM((rows + 2 * halo, (chunks + 2) * 2 * width), bf16),
            pltpu.VMEM((4 * rows, (chunks + 2) * width), bf16),
            pltpu.VMEM((rows, width), f32),
            pltpu.VMEM((levels_w, seg_dev, SEG, cols), f32),
            pltpu.VMEM((rows, levels_e * bands // 8, 8, cols), f32),
            pltpu.VMEM((chunks, seg_dev, seg_rows, width), bf16),
            pltpu.VMEM((chunks, side_count * CAP * seg_rows, width), bf16),
            pltpu.VMEM((chunks, side_count * CAP * seg_rows, width), bf16),
            pltpu.VMEM((side_count, 8, CAP * seg_rows), f32),
            dma((7,)),
            dma((2,)),
            dma((2, pieces)),
            dma((2,)),
            dma((2,)),
            dma,
            dma,
            dma,
            dma((chunks,)),
        ],
        compiler_params=pltpu.CompilerParams(
            collective_id=0, has_side_effects=True, vmem_limit_bytes=44 * 1024 * 1024
        ),
        name="main",
    )(
        *(
            pltpu.with_memory_space_constraint(value, pltpu.HBM)
            for value in (
                routes.T,
                starts.T,
                toa_bands,
                dark_mask,
                kernel[None],
                table(lut_gain),
                table(lut_path),
                table(lut_albedo),
                vapour,
                elev_class,
                elev_frac,
            )
        ),
    )
    out = pl.pallas_call(
        functools.partial(store_kernel, bands),
        out_shape=made[0],
        in_specs=[vmem] * 4,
        out_specs=hbm,
        scratch_shapes=[
            pltpu.VMEM((rows, bands, rest), bf16),
            dma((2,)),
        ],
        name="store",
    )(*(pltpu.with_memory_space_constraint(value, pltpu.VMEM) for value in parts))
    return out[None]


def solution(mesh):
    in_specs = (
        P(("groups", "along"), None, "across"),
        P(("groups", "along"), "across"),
        P(("groups", "along"), "across"),
        P(("groups", "along"), "across"),
        P(("groups", "along"), "across"),
        P(),
        P(),
        P(),
        P(),
        P(("groups", "along"), None),
        P(("groups", "along"), None),
    )
    out_specs = P(("groups", "along"), None, None, "across")
    run = functools.partial(body, mesh.shape["along"], mesh.shape["across"])
    return jax.shard_map(run, mesh=mesh, in_specs=in_specs, out_specs=out_specs, check_vma=False)
```

```python
import functools
import math

import jax
import jax.numpy as jnp
from jax import lax
from jax.experimental import pallas as pl
from jax.experimental.pallas import tpu as pltpu
from jax.sharding import PartitionSpec as P

SEG = 16
REACH = 2
CAP = 2
LANES = 128
WIDTH = 128
MESH_ID = pl.DeviceIdType.MESH
SIDES = [side - REACH for side in range(REACH)] + [side + 1 for side in range(REACH)]
EARLY = 5
DEFER = 4
f32 = jnp.float32
bf16 = jnp.bfloat16


def split(value):
    high = value.astype(bf16)
    return high, (value - high.astype(f32)).astype(bf16)


def toeplitz(taps, row_count, width, first):
    line = jnp.broadcast_to(taps, (8, taps.shape[1]))
    if width > taps.shape[1]:
        line = jnp.concatenate([line, jnp.zeros((8, width - taps.shape[1]), f32)], axis=1)
    stair = pltpu.roll(line, 0, 1, stride=1, stride_axis=0)
    return jnp.concatenate(
        [pltpu.roll(stair, first + 8 * group, 1) for group in range(row_count // 8)], axis=0
    )


def dot_nt(left, right):
    return lax.dot_general(left, right, (((1,), (1,)), ((), ())), preferred_element_type=f32)


def averages(place, segments, scale, bands):
    width = scale.shape[1]
    summed = jnp.dot(place, segments, preferred_element_type=f32)
    for k in range(segments.shape[1] // width):
        result = summed[:, k * width : (k + 1) * width] / scale
        yield result.reshape(-1, bands, width).astype(bf16)


def exists(position, count):
    return (position >= 0) & (position < count)


def main_kernel(
    n_along,
    n_across,
    bands,
    levels,
    routes_hbm,
    starts_hbm,
    toa_hbm,
    mask_hbm,
    taps_hbm,
    gain_hbm,
    path_hbm,
    albedo_hbm,
    vapour_hbm,
    class_hbm,
    frac_hbm,
    out_ref,
    rest_ref,
    place,
    scale,
    routes_ref,
    starts_ref,
    raw_ref,
    mask_ref,
    taps_ref,
    gain_ref,
    path_ref,
    albedo_ref,
    vapour_ref,
    class_ref,
    frac_ref,
    toa_ref,
    tags_ref,
    taps_pad,
    padded,
    tall,
    pos_ref,
    weights,
    heights,
    corrected,
    slots,
    got_rows,
    got_tags,
    load_sem,
    halo_send,
    halo_recv,
    side_send,
    side_recv,
    tag_send,
    tag_recv,
    slot_send,
    slot_recv,
):
    along, across = lax.axis_index("along"), lax.axis_index("across")
    levels_e, levels_a, levels_w = levels
    rows, _, cols = toa_hbm.shape
    halo = (padded.shape[0] - rows) // 2
    half = taps_hbm.shape[1] // 2
    width = slots.shape[2]
    chunks = cols // width
    seg_rows = SEG * bands
    seg_dev = rows // SEG
    own_rows = rows * bands
    pair = 2 * width
    mirror = across % 2
    inner = across + 1 - 2 * mirror
    outer = across - 1 + 2 * mirror
    pieces = halo_recv.shape[1]
    per_piece = chunks // pieces

    def lanes_of(chunk):
        at = jnp.where(mirror == 0, chunk, chunks - 1 - chunk) * width
        return pl.ds(pl.multiple_of(at, width), width)

    loads = [
        pltpu.make_async_copy(source, target, load_sem.at[number if number < 4 else number - 4])
        for number, (source, target) in enumerate(
            (
                (routes_hbm, routes_ref),
                (starts_hbm, starts_ref),
                (toa_hbm, raw_ref),
                (mask_hbm, mask_ref),
                (taps_hbm, taps_ref),
                (gain_hbm, gain_ref),
                (path_hbm, path_ref),
                (albedo_hbm, albedo_ref),
                (vapour_hbm, vapour_ref),
                (class_hbm, class_ref),
                (frac_hbm, frac_ref),
            )
        )
    ]
    for load in loads[:4]:
        load.start()
    barrier = pltpu.get_barrier_semaphore()
    peers = [
        (exists(along + da, n_along), {"along": along + da})
        for da in sorted({-1, 1, *SIDES}, key=abs)
    ]
    peers += [
        (exists(inner, n_across), {"across": inner}),
        (exists(outer, n_across), {"across": outer}),
    ]
    for present, peer in peers:

        @pl.when(present)
        def _():
            pl.semaphore_signal(barrier, inc=1, device_id=peer, device_id_type=MESH_ID)

    row = lax.broadcasted_iota(jnp.int32, (rows, rows * bands), 0) * bands
    col = lax.broadcasted_iota(jnp.int32, (rows, rows * bands), 1)
    pick = jnp.where(col == row, 8.0, 0.0) + jnp.where(col == row + 2, -4.0, 0.0)
    for load in loads[:4]:
        load.wait()
    for load in loads[4:]:
        load.start()
    flat = raw_ref[...].astype(f32).reshape(rows * bands, cols).astype(bf16)
    toa_ref[...] = flat
    value = jnp.dot(pick.astype(bf16), flat, preferred_element_type=f32)
    darkness = mask_ref[...].astype(f32)
    weighted = (darkness * value).astype(bf16)
    darkness = darkness.astype(bf16)
    for tile in range(chunks):
        own = slice(tile * width, (tile + 1) * width)
        at = pl.multiple_of((jnp.where(mirror == 0, tile, chunks - 1 - tile) + 1) * pair, pair)
        padded[halo : halo + rows, pl.ds(at, width)] = weighted[:, own]
        padded[halo : halo + rows, pl.ds(at + width, width)] = darkness[:, own]

    lane = lax.broadcasted_iota(jnp.int32, (8, CAP * seg_rows), 1)
    for number, side in enumerate(SIDES):
        target = jnp.full((8, CAP * seg_rows), -1, jnp.int32)
        rank = jnp.int32(0)
        for s in range(seg_dev):
            hit = routes_ref[1, s] - along == side
            spot = jnp.where(hit, rank, -1)
            inside = (lane >= spot * seg_rows) & (lane < (spot + 1) * seg_rows) & (spot >= 0)
            target = jnp.where(inside, starts_ref[1, s] * bands + lane - spot * seg_rows, target)
            rank = rank + jnp.where(hit, 1, 0)
        tags_ref[number] = target.astype(f32)

    spans = {
        -1: (slice(halo, 2 * halo), slice(halo + rows, 2 * halo + rows)),
        1: (slice(rows, halo + rows), slice(0, halo)),
    }

    def halo_copy(index, piece):
        da = (-1, 1)[index]
        begin = (1 + piece * per_piece) * pair
        at = slice(begin, begin + per_piece * pair)
        return pltpu.make_async_remote_copy(
            src_ref=padded.at[spans[da][0], at],
            dst_ref=padded.at[spans[da][1], at],
            send_sem=halo_send.at[index],
            recv_sem=halo_recv.at[index, piece],
            device_id={"along": along + da},
            device_id_type=MESH_ID,
        )

    def halo_whole(index):
        da = (-1, 1)[index]
        at = slice(pair, (1 + chunks) * pair)
        return pltpu.make_async_remote_copy(
            src_ref=padded.at[spans[da][0], at],
            dst_ref=padded.at[spans[da][1], at],
            send_sem=halo_send.at[index],
            recv_sem=halo_recv.at[index, 0],
            device_id={"along": along + da},
            device_id_type=MESH_ID,
        )

    def side_copy(index):
        source, target = ((chunks, chunks + 1), (1, 0))[index]
        return pltpu.make_async_remote_copy(
            src_ref=padded.at[:, source * pair : (source + 1) * pair],
            dst_ref=padded.at[:, target * pair : (target + 1) * pair],
            send_sem=side_send.at[index],
            recv_sem=side_recv.at[index],
            device_id={"across": (inner, outer)[index]},
            device_id_type=MESH_ID,
        )

    def tag_copy(number):
        return pltpu.make_async_remote_copy(
            src_ref=tags_ref.at[number],
            dst_ref=got_tags.at[number],
            send_sem=tag_send,
            recv_sem=tag_recv,
            device_id={"along": along + SIDES[number]},
            device_id_type=MESH_ID,
        )

    def slot_copy(chunk, number):
        count = CAP * seg_rows
        return pltpu.make_async_remote_copy(
            src_ref=slots.at[chunk, number * count : (number + 1) * count],
            dst_ref=got_rows.at[chunk, number * count : (number + 1) * count],
            send_sem=slot_send,
            recv_sem=slot_recv.at[chunk],
            device_id={"along": along + SIDES[number]},
            device_id_type=MESH_ID,
        )

    def count_of(flags):
        return sum(flag.astype(jnp.int32) for flag in flags)

    half_count = len(SIDES) // 2
    gone = [exists(along + side, n_along) for side in SIDES]
    come = [exists(along - side, n_along) for side in SIDES]
    gone_first = half_count - count_of(gone[:half_count])
    come_first = half_count - count_of(come[:half_count])
    gone_count, come_count = count_of(gone), count_of(come)
    per_side = CAP * seg_rows

    def tags_wait(first, count, sent):
        for k in range(1, len(SIDES) + 1):

            @pl.when(count == k)
            def _():
                copy = pltpu.make_async_remote_copy(
                    src_ref=tags_ref.at[pl.ds(first, k)],
                    dst_ref=got_tags.at[pl.ds(first, k)],
                    send_sem=tag_send,
                    recv_sem=tag_recv,
                    device_id={"along": along},
                    device_id_type=MESH_ID,
                )
                if sent:
                    copy.wait_send()
                else:
                    copy.wait_recv()

    def slots_wait(first, count, chunk):
        for k in range(1, len(SIDES) + 1):

            @pl.when(count == k)
            def _():
                at = pl.ds(pl.multiple_of(first * per_side, per_side), k * per_side)
                which = slice(0, chunks) if chunk is None else chunk
                copy = pltpu.make_async_remote_copy(
                    src_ref=slots.at[which, at],
                    dst_ref=got_rows.at[which, at],
                    send_sem=slot_send,
                    recv_sem=slot_recv.at[0 if chunk is None else chunk],
                    device_id={"along": along},
                    device_id_type=MESH_ID,
                )
                if chunk is None:
                    copy.wait_send()
                else:
                    copy.wait_recv()

    def start_halo(piece):
        for index, da in enumerate((-1, 1)):

            @pl.when(exists(along + da, n_along))
            def _():
                halo_copy(index, piece).start()

    pl.semaphore_wait(barrier, sum(present.astype(jnp.int32) for present, _ in peers))
    start_halo(0)
    order = sorted(range(len(SIDES)), key=lambda number: abs(SIDES[number]))
    for number in order:

        @pl.when(exists(along + SIDES[number], n_along))
        def _():
            tag_copy(number).start()

        @pl.when(jnp.logical_not(exists(along - SIDES[number], n_along)))
        def _():
            begin = number * CAP * seg_rows
            got_rows[:, begin : begin + CAP * seg_rows, :] = jnp.zeros(
                (chunks, CAP * seg_rows, width), bf16
            )
            got_tags[number] = jnp.full(got_tags.shape[1:], -1.0, f32)

    for da in (-1, 1):

        @pl.when(jnp.logical_not(exists(along - da, n_along)))
        def _():
            padded[spans[da][1], pair : (chunks + 1) * pair] = jnp.zeros(
                (halo, chunks * pair), bf16
            )

    for index, (peer, target) in enumerate(((inner, chunks + 1), (outer, 0))):

        @pl.when(jnp.logical_not(exists(peer, n_across)))
        def _():
            padded[:, target * pair : (target + 1) * pair] = jnp.zeros(
                (padded.shape[0], pair), bf16
            )

    for load in loads[4:8]:
        load.wait()
    taps_pad[...] = jnp.zeros(taps_pad.shape, f32)
    taps_pad[0:1, 0 : taps_ref.shape[1]] = taps_ref[...]
    taps = taps_pad[0:1, :]
    down = jnp.concatenate(split(toeplitz(taps, rows, 2 * halo + rows, halo - half)), axis=0)
    wide = toeplitz(taps, width, 3 * width, width - half)
    turned = jnp.concatenate(
        [wide[:, (2 - k) * width : (3 - k) * width] for k in range(3)], axis=1
    )
    sideways = jnp.concatenate(split(jnp.where(mirror == 0, wide, turned)), axis=0)

    node_count = levels_w * levels_a
    tables = jnp.concatenate([gain_ref[...], path_ref[...], albedo_ref[...]], axis=0)
    spread_a = lax.broadcasted_iota(jnp.int32, (levels_a, node_count), 0)
    spread_n = lax.broadcasted_iota(jnp.int32, (levels_a, node_count), 1)
    spread = jnp.where(spread_n % levels_a == spread_a, 1.0, 0.0).astype(bf16)
    wide = jnp.dot(tables, spread, preferred_element_type=f32)
    wide_w = lax.broadcasted_iota(jnp.int32, wide.shape, 0) % levels_w
    wide_n = lax.broadcasted_iota(jnp.int32, wide.shape, 1) // levels_a
    wide = jnp.where(wide_w == wide_n, wide, 0.0).astype(bf16)
    table_rows = levels_e * bands
    into = lax.broadcasted_iota(jnp.int32, (3 * table_rows, wide.shape[0]), 0)
    source = lax.broadcasted_iota(jnp.int32, (3 * table_rows, wide.shape[0]), 1) // levels_w
    within = into % table_rows
    wanted = into - within + (within % bands) * levels_e + within // bands
    lut = jnp.dot(
        jnp.where(source == wanted, 1.0, 0.0).astype(bf16), wide, preferred_element_type=f32
    ).astype(bf16)

    for load in loads[8:]:
        load.wait()
    sub = lax.broadcasted_iota(jnp.int32, (8, width), 0)
    lower = sub < bands
    pair_e = (sub // bands).astype(f32)
    per_tile = 8 // bands

    def prepare(index, carry):
        at_cols = pl.ds(pl.multiple_of((index // seg_dev) * width, width), width)
        base = pl.multiple_of((index % seg_dev) * SEG, SEG)
        at_rows = pl.ds(base, SEG)
        vapour = vapour_ref[at_rows, at_cols]
        height = class_ref[at_rows, at_cols].astype(f32) + frac_ref[at_rows, at_cols]
        for w in range(levels_w):
            weights[w, index % seg_dev, :, at_cols] = jnp.maximum(0.0, 1.0 - jnp.abs(vapour - float(w)))
        for row in range(SEG):
            for k in range(table_rows // 8):
                heights[base + row, k, :, at_cols] = jnp.maximum(
                    0.0, 1.0 - jnp.abs(height[row : row + 1] - (pair_e + float(per_tile * k)))
                )
        return carry

    early = seg_dev * chunks * EARLY // 16
    lax.fori_loop(0, early, prepare, 0)
    if pieces > 1:
        start_halo(1)
    lax.fori_loop(early, seg_dev * chunks, prepare, 0)
    if pieces > 2:
        start_halo(2)

    def wait_piece(piece):
        for index, da in enumerate((-1, 1)):

            @pl.when(exists(along - da, n_along))
            def _():
                halo_copy(index, piece).wait_recv()

    def start_side(index):
        @pl.when(exists((inner, outer)[index], n_across))
        def _():
            side_copy(index).start()

    def wait_side(index):
        @pl.when(exists((inner, outer)[index], n_across))
        def _():
            side_copy(index).wait_recv()

    def fall(tile):
        product = jnp.dot(
            down, padded[:, tile * pair : (tile + 1) * pair], preferred_element_type=f32
        )
        high, low = split(product[:rows] + product[rows:])
        at = slice(tile * width, (tile + 1) * width)
        tall[0:rows, at] = high[:, :width]
        tall[rows : 2 * rows, at] = high[:, width:]
        tall[2 * rows : 3 * rows, at] = low[:, :width]
        tall[3 * rows : 4 * rows, at] = low[:, width:]

    def smooth(chunk):
        fresh = [chunk + 2] if chunk else [1, 2, 0]
        for tile in fresh:
            if tile == 0:
                wait_side(1)
            elif tile == chunks + 1:
                wait_side(0)
            elif (tile - 1) % per_piece == 0:
                wait_piece((tile - 1) // per_piece)
                if tile == 1:
                    start_side(1)
                if tile + per_piece == chunks + 1:
                    start_side(0)
            fall(tile)
        product = dot_nt(tall[:, chunk * width : (chunk + 3) * width], sideways)
        smoothed = product[: 2 * rows, :width] + (
            product[2 * rows :, :width] + product[: 2 * rows, width:]
        )
        aerosol = smoothed[:rows] / jnp.maximum(smoothed[rows:], 1.0)
        pos_ref[...] = (levels_a - 1) * jax.nn.sigmoid(aerosol)

    chosen = []
    for number, side in enumerate(SIDES):
        rank = jnp.int32(0)
        first = [jnp.int32(0) for _ in range(CAP)]
        for s in range(seg_dev):
            hit = routes_ref[1, s] - along == side
            for k in range(CAP):
                first[k] = jnp.where(hit & (rank == k), s, first[k])
            rank = rank + jnp.where(hit, 1, 0)
        chosen.append(first)

    node_a = lax.broadcasted_iota(jnp.int32, (levels_a, width), 0).astype(f32)
    quad = 16 // bands
    group = max(1, 256 // width)

    def correct(chunk, seg):
        at_cols = lanes_of(chunk)
        base = pl.multiple_of(seg * SEG, SEG)
        base_flat = pl.multiple_of(seg * seg_rows, seg_rows)
        position = pos_ref[pl.ds(base, SEG), :]
        for first in range(0, SEG, quad):
            partial = []
            values = []
            for start in range(first, first + quad, group):
                joints = []
                for row in range(start, start + group):
                    weight_a = jnp.maximum(0.0, 1.0 - jnp.abs(position[row : row + 1] - node_a))
                    weight_a = weight_a.astype(bf16)
                    joints.append(
                        jnp.concatenate(
                            [
                                weight_a
                                * jnp.broadcast_to(
                                    weights[w, seg, row : row + 1, at_cols], (levels_a, width)
                                ).astype(bf16)
                                for w in range(levels_w)
                            ],
                            axis=0,
                        )
                    )
                joint = joints[0] if group == 1 else jnp.concatenate(joints, axis=1)
                product = jnp.dot(lut, joint, preferred_element_type=f32)
                for k in range(group):
                    values.append(product[:, k * width : (k + 1) * width])
            for row in range(first, first + quad):
                nodes = values[row - first]
                sums = [None] * 3
                for k in range(table_rows // 8):
                    weight_e = heights[base + row, k, :, at_cols]
                    for t in range(3):
                        at = t * table_rows + k * 8
                        term = nodes[at : at + 8] * weight_e
                        sums[t] = term if sums[t] is None else sums[t] + term
                partial.append(sums)
            radiance = toa_ref[pl.ds(base_flat + first * bands, quad * bands), at_cols].astype(f32)
            surfaces = []
            for part in range(quad // 2):
                coefficient = []
                for t in range(3):
                    one, two = partial[2 * part][t], partial[2 * part + 1][t]
                    kept = jnp.where(lower, one, two)
                    moved = pltpu.roll(jnp.where(lower, two, one), bands, 0)
                    coefficient.append(kept + moved)
                scaled = coefficient[0] * radiance[part * 8 : part * 8 + 8] - coefficient[1]
                surfaces.append(scaled / (1.0 + coefficient[2] * scaled))
            corrected[chunk, seg, first * bands : (first + quad) * bands, :] = jnp.concatenate(
                surfaces, axis=0
            ).astype(bf16)

    def correct_all(chunk):
        def step(seg, carry):
            correct(chunk, seg)
            return carry

        lax.fori_loop(0, seg_dev, step, 0, unroll=True)

    def fill_slots(chunk):
        for number in range(len(SIDES)):
            for k in range(CAP):
                into = (number * CAP + k) * seg_rows
                slots[chunk, into : into + seg_rows] = corrected[chunk, chosen[number][k]]

    def start_slot(chunk, number, wanted):
        @pl.when(exists(along + SIDES[number], n_along) & wanted)
        def _():
            slot_copy(chunk, number).start()

    odd = along % 2 == 1
    even = jnp.logical_not(odd)
    near = {number: odd if side < 0 else even for number, side in enumerate(SIDES)}

    def start_slots(chunk):
        for number, side in enumerate(SIDES):
            if abs(side) == 1:
                start_slot(chunk, number, near[number])
        for number, side in enumerate(SIDES):
            if abs(side) != 1:
                start_slot(chunk, number, True)
        if chunk >= 1:
            start_far(chunk - 1, mirror != 0)
        if chunk >= DEFER:
            start_far(chunk - DEFER, mirror == 0)

    def start_far(chunk, wanted):
        for number, side in enumerate(SIDES):
            if abs(side) == 1:
                start_slot(chunk, number, jnp.logical_not(near[number]) & wanted)

    def placed(target):
        row = lax.broadcasted_iota(jnp.int32, (own_rows, target.shape[1]), 0).astype(f32)
        return jnp.where(row == target, 1.0, 0.0).astype(bf16)

    def make_place():
        lane = lax.broadcasted_iota(jnp.int32, (1, own_rows), 1)
        target = jnp.full((1, own_rows), -1, jnp.int32)
        for s in range(seg_dev):
            inside = (lane >= s * seg_rows) & (lane < (s + 1) * seg_rows)
            inside = inside & (routes_ref[0, s] == along)
            target = jnp.where(inside, starts_ref[0, s] * bands + lane - s * seg_rows, target)
        place[:, 0:own_rows] = placed(target.astype(f32))
        tags_wait(come_first, come_count, False)
        for number in order:
            begin = own_rows + number * CAP * seg_rows
            place[:, begin : begin + CAP * seg_rows] = placed(got_tags[number, 0:1, :])
        ones = jnp.ones((place.shape[1], width), bf16)
        count = jnp.dot(place[...], ones, preferred_element_type=f32)
        scale[...] = jnp.maximum(count, 1.0)

    def arrived(first, count):
        for chunk in range(first, first + count):
            slots_wait(come_first, come_count, chunk)

    def put(first, count):
        arrived(first, count)
        segments = [
            jnp.concatenate([corrected[chunk].reshape(own_rows, width), got_rows[chunk]], axis=0)
            for chunk in range(first, first + count)
        ]
        segments = segments[0] if count == 1 else jnp.concatenate(segments, axis=1)
        for k, result in enumerate(averages(place[...], segments, scale[...], bands)):
            out_ref[:, :, lanes_of(first + k)] = result

    for chunk in range(chunks):
        smooth(chunk)
        if chunk > 1:
            start_slots(chunk - 1)
        correct_all(chunk)
        if chunk == 0:
            for piece in range(3, pieces):
                start_halo(piece)
        fill_slots(chunk)
        if chunk == 0:
            make_place()
            if chunks > 1:
                start_slots(0)
    start_slots(chunks - 1)
    start_far(chunks - 1, mirror != 0)
    for chunk in range(chunks - min(DEFER, chunks), chunks):
        start_far(chunk, mirror == 0)
    rest = rest_ref.shape[1] // width
    for k in range(rest):
        mine = corrected[chunks - rest + k].reshape(own_rows, width)
        rest_ref[0:own_rows, k * width : (k + 1) * width] = mine
    for first in range(0, chunks - rest, 2):
        put(first, min(2, chunks - rest - first))
    arrived(chunks - rest, rest)
    for k in range(rest):
        rest_ref[own_rows:, k * width : (k + 1) * width] = got_rows[chunks - rest + k]

    for index, da in enumerate((-1, 1)):

        @pl.when(exists(along + da, n_along))
        def _():
            halo_whole(index).wait_send()

    for index, peer in enumerate((inner, outer)):

        @pl.when(exists(peer, n_across))
        def _():
            side_copy(index).wait_send()

    tags_wait(gone_first, gone_count, True)
    slots_wait(gone_first, gone_count, None)


def store_kernel(bands, done_ref, rest_ref, place, scale, out_hbm, last, sem):
    rows, _, cols = out_hbm.shape
    width = scale.shape[1]
    rest = rest_ref.shape[1]
    mirror = lax.axis_index("across") % 2
    at = pl.ds(pl.multiple_of(jnp.where(mirror == 0, 0, rest), width), cols - rest)
    parts = sem.shape[0] - 1
    copies = []
    for part in range(parts):
        own = slice(part * rows // parts, (part + 1) * rows // parts)
        copies.append(
            pltpu.make_async_copy(done_ref.at[own, :, at], out_hbm.at[own, :, at], sem.at[part])
        )
    if rest < cols:
        for copy in copies:
            copy.start()
    pieces = averages(place[...], rest_ref[...], scale[...], bands)
    for k, result in enumerate(pieces):
        spot = jnp.where(mirror == 0, k, rest // width - 1 - k) * width
        last[:, :, pl.ds(pl.multiple_of(spot, width), width)] = result
    at = pl.ds(pl.multiple_of(jnp.where(mirror == 0, cols - rest, 0), width), rest)
    final = pltpu.make_async_copy(last, out_hbm.at[:, :, at], sem.at[parts])
    final.start()
    if rest < cols:
        for copy in copies:
            copy.wait()
    final.wait()


def body(
    n_along,
    n_across,
    toa_bands,
    dark_mask,
    vapour,
    elev_class,
    elev_frac,
    kernel,
    lut_gain,
    lut_path,
    lut_albedo,
    routes,
    starts,
):
    rows, bands, cols = toa_bands.shape
    half = kernel.shape[0] // 2
    halo = -(-half // 16) * 16
    levels = lut_gain.shape[1:]
    levels_e, levels_a, levels_w = levels
    seg_dev = routes.shape[0]
    seg_rows = SEG * bands
    side_count = len(SIDES)
    width = math.gcd(cols, WIDTH)
    chunks = cols // width
    pieces = chunks // math.gcd(chunks, 2)
    vmem = pl.BlockSpec(memory_space=pltpu.VMEM)
    hbm = pl.BlockSpec(memory_space=pltpu.HBM)
    table_shape = (bands * levels_e * levels_w, levels_a)
    dma = pltpu.SemaphoreType.DMA

    def table(lut):
        return lut.transpose(0, 1, 3, 2).reshape(table_shape)

    rest = width
    held = (rows * bands, rows * bands + side_count * CAP * seg_rows)
    made = (
        jax.ShapeDtypeStruct((rows, bands, cols), bf16),
        jax.ShapeDtypeStruct((held[1], rest), bf16),
        jax.ShapeDtypeStruct(held, bf16),
        jax.ShapeDtypeStruct((rows * bands, width), f32),
    )
    parts = pl.pallas_call(
        functools.partial(main_kernel, n_along, n_across, bands, levels),
        out_shape=made,
        in_specs=[hbm] * 11,
        out_specs=[vmem] * 4,
        scratch_shapes=[
            pltpu.SMEM((2, seg_dev), jnp.int32),
            pltpu.SMEM((2, seg_dev), jnp.int32),
            pltpu.VMEM((rows, bands, cols), bf16),
            pltpu.VMEM((rows, cols), jnp.int32),
            pltpu.VMEM((1, kernel.shape[0]), f32),
            pltpu.VMEM(table_shape, bf16),
            pltpu.VMEM(table_shape, bf16),
            pltpu.VMEM(table_shape, bf16),
            pltpu.VMEM((rows, cols), f32),
            pltpu.VMEM((rows, cols), jnp.int32),
            pltpu.VMEM((rows, cols), f32),
            pltpu.VMEM((rows * bands, cols), bf16),
            pltpu.VMEM((side_count, 8, CAP * seg_rows), f32),
            pltpu.VMEM((8, LANES), f32),
            pltpu.VMEM((rows + 2 * halo, (chunks + 2) * 2 * width), bf16),
            pltpu.VMEM((4 * rows, (chunks + 2) * width), bf16),
            pltpu.VMEM((rows, width), f32),
            pltpu.VMEM((levels_w, seg_dev, SEG, cols), f32),
            pltpu.VMEM((rows, levels_e * bands // 8, 8, cols), f32),
            pltpu.VMEM((chunks, seg_dev, seg_rows, width), bf16),
            pltpu.VMEM((chunks, side_count * CAP * seg_rows, width), bf16),
            pltpu.VMEM((chunks, side_count * CAP * seg_rows, width), bf16),
            pltpu.VMEM((side_count, 8, CAP * seg_rows), f32),
            dma((7,)),
            dma((2,)),
            dma((2, pieces)),
            dma((2,)),
            dma((2,)),
            dma,
            dma,
            dma,
            dma((chunks,)),
        ],
        compiler_params=pltpu.CompilerParams(
            collective_id=0, has_side_effects=True, vmem_limit_bytes=44 * 1024 * 1024
        ),
        name="main",
    )(
        *(
            pltpu.with_memory_space_constraint(value, pltpu.HBM)
            for value in (
                routes.T,
                starts.T,
                toa_bands,
                dark_mask,
                kernel[None],
                table(lut_gain),
                table(lut_path),
                table(lut_albedo),
                vapour,
                elev_class,
                elev_frac,
            )
        ),
    )
    out = pl.pallas_call(
        functools.partial(store_kernel, bands),
        out_shape=made[0],
        in_specs=[vmem] * 4,
        out_specs=hbm,
        scratch_shapes=[
            pltpu.VMEM((rows, bands, rest), bf16),
            dma((2,)),
        ],
        name="store",
    )(*(pltpu.with_memory_space_constraint(value, pltpu.VMEM) for value in parts))
    return out[None]


def solution(mesh):
    in_specs = (
        P(("groups", "along"), None, "across"),
        P(("groups", "along"), "across"),
        P(("groups", "along"), "across"),
        P(("groups", "along"), "across"),
        P(("groups", "along"), "across"),
        P(),
        P(),
        P(),
        P(),
        P(("groups", "along"), None),
        P(("groups", "along"), None),
    )
    out_specs = P(("groups", "along"), None, None, "across")
    run = functools.partial(body, mesh.shape["along"], mesh.shape["across"])
    return jax.shard_map(run, mesh=mesh, in_specs=in_specs, out_specs=out_specs, check_vma=False)
```
